512 devices in a mesh: head: 8 (over y, x_hi), seq: 64 (over z, x_lo, core).
Axes of the slice: x: 4 (x_hi: 2, x_lo: 2; x = x_hi * 2 + x_lo), y: 4, z: 16, core: 2. Of those that a mesh axis runs over, the one named last changes fastest.
Arguments:
- tokens: bfloat16 [49152, 2048], P('seq', 'head'), may hold values from -6 to 6
- weights: bfloat16 [3, 2048, 2048], P(None, 'seq', 'head'), may hold values from -0.06591797 to 0.06591797
- landmark_pos: int32 [16, 256], P('head'), may hold values from 0 to 49151, as said below
Outputs:
- attended: bfloat16 [49152, 2048], P('seq', 'head')
The draws below stay inside these ranges and needn't reach their ends.
Inputs may be any that keep to these rules, and one draw needn't show every extreme that they name: `landmark_pos`: landmark number j of every head lies in tokens j * 192 to (j + 1) * 192 - 1.
All inputs are finite; a program needn't handle non-finite values. Where the reference program divides by a largest or mean magnitude, that divisor is 1e-20 or more.
Results may differ from the reference program's by a relative error of at most 0.0041.
Values may be sent and summed in bfloat16 or wider, within the bound.
No kernel may reach another device: no remote copies, remote signals or barrier semaphores. Data moves between devices by JAX's collectives and lax.ppermute only.
A program may use at most 64 MiB of HBM per device.

```python
import math
import jax
import jax.numpy as jnp
from jax import lax

D = 2048
H = 16
E = 128
M = 256
NSTEPS = 6
SEQ_LEN = 49152


def draw_landmark_pos(key, part):
    offsets = jax.random.randint(key, (H, M), 0, SEQ_LEN // M)
    offsets = offsets.at[0, 0].set(0).at[0, M - 1].set(SEQ_LEN // M - 1)
    starts = jnp.arange(M, dtype=jnp.int32)[None, :] * (SEQ_LEN // M)
    return (starts + offsets).astype(jnp.int32)


def draw_tokens(key, part):
    noise_key = jax.random.fold_in(key, 11)
    block_key = jax.random.fold_in(key, 12)
    noise = jax.random.normal(noise_key, (SEQ_LEN, D), jnp.float32)
    shared = jax.random.normal(block_key, (M, D), jnp.float32)
    whole = noise + jnp.repeat(shared, SEQ_LEN // M, axis=0)
    return jnp.clip(whole, -6.0, 6.0).astype(jnp.bfloat16)


def levels(stream_key, shape, shards, least, top_value):
    gain, own = 1.0, jax.random.fold_in(stream_key, 6)
    for position, blocks in shards:
        draws = jnp.exp(jax.random.uniform(jax.random.fold_in(own, position), (blocks,), jnp.float32, least / len(shards), top_value / len(shards)))
        gain = gain * jnp.repeat(draws, shape[position] // blocks).reshape([-1 if axis == position else 1 for axis in range(len(shape))])
    return gain


def normal_values(stream_key, dims, width, most, pieces=(), kind=jnp.bfloat16):
    values = width * jax.random.normal(stream_key, dims, jnp.float32)
    if pieces:
        values = values * levels(stream_key, dims, pieces, -0.22, 0.18)
    return jnp.clip(values, -most, most).astype(kind)


def setup_inputs(seed: int = 0) -> dict:
    streams_of = jax.random.split(jax.random.key(seed), 4)
    tokens = draw_tokens(jax.random.fold_in(streams_of[3], 71), 0)
    weights = normal_values(streams_of[1], (3, D, H * E), (0.45 * D ** -0.5), 0.06591797, ((1, 64), (2, 8)))
    landmark_pos = draw_landmark_pos(jax.random.fold_in(streams_of[3], 71), 0)
    return {"tokens": tokens, "weights": weights, "landmark_pos": landmark_pos}


def gauss(left, right):
    left32 = left.astype(jnp.float32)
    right32 = right.astype(jnp.float32)
    inner = jnp.einsum('ie,je->ij', left32, right32)
    dist = lax.optimization_barrier(jnp.sum(left32 * left32, -1))[:, None] + lax.optimization_barrier(jnp.sum(right32 * right32, -1))[None, :] - 2.0 * inner
    return jnp.exp(-dist / (2.0 * math.sqrt(left.shape[-1])))

def one_head(packed):
    query, keys, values, places = packed
    even = (jnp.arange(M) % 2 == 0)[:, None]
    landmarks = jnp.where(even, query[places], keys[places])
    inner = gauss(landmarks, landmarks)
    key_weights = gauss(landmarks, keys).astype(jnp.bfloat16)
    summary = jnp.dot(key_weights, values, preferred_element_type=jnp.float32)
    scale_cols = jnp.max(lax.optimization_barrier(jnp.sum(jnp.abs(inner), 0)))
    scale_rows = jnp.max(lax.optimization_barrier(jnp.sum(jnp.abs(inner), 1)))
    iterate = inner / (scale_cols * scale_rows)
    for step in range(NSTEPS):
        left = jnp.dot(iterate, inner, precision=lax.Precision.HIGHEST)
        iterate = 2.0 * iterate - jnp.dot(left, iterate, precision=lax.Precision.HIGHEST)
    mixed = jnp.dot(iterate, summary, precision=lax.Precision.HIGHEST).astype(jnp.bfloat16)
    query_weights = gauss(query, landmarks).astype(jnp.bfloat16)
    return jnp.dot(query_weights, mixed, preferred_element_type=jnp.float32).astype(jnp.bfloat16)

def reference(tokens, weights, landmark_pos):

    def project(index):
        flat = jnp.dot(tokens, weights[index], preferred_element_type=jnp.float32).astype(jnp.bfloat16)
        return jnp.transpose(flat.reshape(SEQ_LEN, H, E), (1, 0, 2))
    query = project(0)
    keys = project(1)
    values = project(2)
    result = lax.map(one_head, (query, keys, values, landmark_pos))
    return jnp.transpose(result, (1, 0, 2)).reshape(SEQ_LEN, H * E)
```

```python
import math

import jax
import jax.numpy as jnp
import numpy as np
from jax import lax
from jax.sharding import Mesh
from jax.sharding import PartitionSpec as P

NSTEPS = 6
AXES = ("y", "xh", "z", "xl", "c")
SIZES = (4, 2, 16, 2, 2)
HEAD = ("y", "xh")
SEQ = ("z", "xl", "c")


def shift(value, axis, step):
    size = lax.axis_size(axis)
    return lax.ppermute(value, axis, [(i, (i + step) % size) for i in range(size)])


def gauss(left, right):
    inner = jnp.einsum("hie,hje->hij", left, right, preferred_element_type=jnp.float32)
    left32 = left.astype(jnp.float32)
    right32 = right.astype(jnp.float32)
    dist = (
        jnp.sum(left32 * left32, -1)[:, :, None]
        + jnp.sum(right32 * right32, -1)[:, None, :]
        - 2.0 * inner
    )
    return jnp.exp(-dist / (2.0 * math.sqrt(left.shape[-1])))


def high(left, right):
    return jnp.dot(left, right, precision=lax.Precision.HIGHEST)


def gather_tokens(own):
    spread = jnp.broadcast_to(own[None], (8,) + own.shape)
    return lax.all_to_all(spread, HEAD, 0, 0, tiled=True)


def gather_weights(own):
    kinds, depth, cols = own.shape
    xl, c = lax.axis_index("xl"), lax.axis_index("c")
    column = lax.all_gather(own, "z", axis=1)
    across = shift(column, "xl", 1)
    core = shift(column, "c", 1)
    both = shift(across, "c", 1)

    def ordered(index, first, second, axis):
        return jnp.where(
            index == 0, jnp.stack([first, second], axis), jnp.stack([second, first], axis)
        )

    rows = ordered(xl, ordered(c, column, core, 2), ordered(c, across, both, 2), 2)
    return rows.reshape(kinds, 8, 256, cols)


def shards(tokens, weights, landmark_pos):
    tok_rows = tokens.shape[0]
    heads_dev = landmark_pos.shape[0]
    head_cols = weights.shape[2]
    head_size = head_cols // heads_dev
    c, xl = lax.axis_index("c"), lax.axis_index("xl")
    group = lax.axis_index(SEQ)
    whole = gather_tokens(tokens)
    gathered = gather_weights(weights)
    projected = jnp.einsum("btd,kbdc->ktc", whole, gathered, preferred_element_type=jnp.float32)

    def heads_of(flat):
        return jnp.transpose(
            flat.astype(jnp.bfloat16).reshape(tok_rows, heads_dev, head_size), (1, 0, 2)
        )

    query, keys, values = heads_of(projected[0]), heads_of(projected[1]), heads_of(projected[2])
    per_group = landmark_pos.shape[1] // 64
    local_pos = lax.dynamic_slice_in_dim(landmark_pos, group * per_group, per_group, 1)
    offsets = local_pos - group * tok_rows
    picker = (offsets[:, :, None] == jnp.arange(tok_rows, dtype=jnp.int32)[None, None, :]).astype(
        jnp.bfloat16
    )
    picked_q = jnp.einsum("hjt,hte->hje", picker, query, preferred_element_type=jnp.float32)
    picked_k = jnp.einsum("hjt,hte->hje", picker, keys, preferred_element_type=jnp.float32)
    even = (jnp.arange(per_group) % 2 == 0)[None, :, None]
    local_marks = jnp.where(even, picked_q, picked_k).astype(jnp.bfloat16)
    block = local_marks.reshape(heads_dev * per_group, head_size)
    spread = jnp.broadcast_to(block[None], (64,) + block.shape)
    marks = lax.all_to_all(spread, SEQ, 0, 0, tiled=True)
    landmarks = jnp.transpose(
        marks.reshape(64, heads_dev, per_group, head_size), (1, 0, 2, 3)
    ).reshape(heads_dev, 64 * per_group, head_size)
    key_weights = gauss(keys, landmarks).astype(jnp.bfloat16)
    partial = jnp.einsum("hte,htj->hej", values, key_weights, preferred_element_type=jnp.float32)
    give = lax.dynamic_index_in_dim(partial, 1 - c, 0, keepdims=False)
    keep = lax.dynamic_index_in_dim(partial, c, 0, keepdims=False)
    mine = lax.dynamic_index_in_dim(landmarks, c, 0, keepdims=True)
    inner = gauss(mine, mine)[0]
    chip = keep + shift(give, "c", 1)
    half = head_size // 2
    give = lax.dynamic_slice_in_dim(chip, (1 - xl) * half, half, 0)
    keep = lax.dynamic_slice_in_dim(chip, xl * half, half, 0)
    quarter = keep + shift(give, "xl", 1)
    scale_cols = jnp.max(jnp.sum(jnp.abs(inner), 0))
    scale_rows = jnp.max(jnp.sum(jnp.abs(inner), 1))
    iterate = inner / (scale_cols * scale_rows)
    for step in range(NSTEPS):
        iterate = 2.0 * iterate - high(high(iterate, inner), iterate)
    pieces = lax.all_gather(quarter.astype(jnp.bfloat16), "z", axis=0)
    summed = jnp.sum(pieces.astype(jnp.float32), 0)
    mixed = lax.dot_general(
        summed, iterate, (((1,), (1,)), ((), ())), precision=lax.Precision.HIGHEST
    ).astype(jnp.bfloat16)
    other = shift(mixed, "xl", 1)
    one = jnp.where(xl == 0, jnp.concatenate([mixed, other], 0), jnp.concatenate([other, mixed], 0))
    two = shift(one, "c", 1)
    mixed_all = jnp.where(c == 0, jnp.stack([one, two]), jnp.stack([two, one]))
    query_weights = gauss(query, landmarks).astype(jnp.bfloat16)
    result = jnp.einsum(
        "htm,hem->the", query_weights, mixed_all, preferred_element_type=jnp.float32
    )
    return result.reshape(tok_rows, head_cols).astype(jnp.bfloat16)


def solution(mesh):
    fine = Mesh(mesh.devices.reshape(SIZES), AXES)
    return jax.shard_map(
        shards,
        mesh=fine,
        in_specs=(P(SEQ, HEAD), P(None, SEQ, HEAD), P(HEAD, None)),
        out_specs=P(SEQ, HEAD),
        check_vma=False,
    )
```

```python
import math

import jax
import jax.numpy as jnp
from jax import lax
from jax.experimental import pallas as pl
from jax.experimental.pallas import tpu as pltpu
from jax.sharding import Mesh
from jax.sharding import PartitionSpec as P

NSTEPS = 6
AXES = ("y", "xh", "z", "xl", "c")
SIZES = (4, 2, 16, 2, 2)
HEAD = ("y", "xh")
SEQ = ("z", "xl", "c")


def shift(value, axis, step):
    size = lax.axis_size(axis)
    return lax.ppermute(value, axis, [(i, (i + step) % size) for i in range(size)])


def gauss(left, right):
    inner = jnp.einsum("hie,hje->hij", left, right, preferred_element_type=jnp.float32)
    left32 = left.astype(jnp.float32)
    right32 = right.astype(jnp.float32)
    dist = (
        jnp.sum(left32 * left32, -1)[:, :, None]
        + jnp.sum(right32 * right32, -1)[:, None, :]
        - 2.0 * inner
    )
    return jnp.exp(-dist / (2.0 * math.sqrt(left.shape[-1])))


def high(left, right):
    return jnp.dot(left, right, precision=lax.Precision.HIGHEST)


def inverse_kernel(marks_ref, inverse_ref):
    marks = marks_ref[...]
    marks32 = marks.astype(jnp.float32)
    squares = marks32 * marks32
    across = (((1,), (1,)), ((), ()))
    product = lax.dot_general(marks, marks, across, preferred_element_type=jnp.float32)
    down_norm = jnp.sum(squares, 1, keepdims=True)
    ones = jnp.ones((8, squares.shape[1]), jnp.float32)
    side_norm = lax.dot_general(
        ones, squares, across, precision=lax.Precision.HIGHEST, preferred_element_type=jnp.float32
    )[:1]
    inner = jnp.exp((down_norm + side_norm - 2.0 * product) * (-0.5 / math.sqrt(marks.shape[1])))
    scale_cols = jnp.max(jnp.sum(jnp.abs(inner), 0, keepdims=True), 1, keepdims=True)
    scale_rows = jnp.max(jnp.sum(jnp.abs(inner), 1, keepdims=True), 0, keepdims=True)
    iterate = inner / (scale_cols * scale_rows)
    for step in range(NSTEPS):
        iterate = 2.0 * iterate - high(high(iterate, inner), iterate)
    inverse_ref[...] = iterate


def invert(marks):
    count = marks.shape[0]
    return pl.pallas_call(
        inverse_kernel,
        out_shape=jax.ShapeDtypeStruct((count, count), jnp.float32),
        in_specs=[pl.BlockSpec(memory_space=pltpu.VMEM)],
        out_specs=pl.BlockSpec(memory_space=pltpu.VMEM),
        cost_estimate=pl.CostEstimate(
            flops=2 * 6 * 12 * count**3, bytes_accessed=4 * count**2, transcendentals=count**2
        ),
        name="inverse",
    )(marks)


def gather_tokens(own):
    spread = jnp.broadcast_to(own[None], (8,) + own.shape)
    return lax.all_to_all(spread, HEAD, 0, 0, tiled=True)


def in_order(column, core, across, both):
    kinds, _, _, cols = column.shape
    xl, c = lax.axis_index("xl"), lax.axis_index("c")

    def ordered(index, first, second):
        return jnp.where(index == 0, jnp.stack([first, second], 2), jnp.stack([second, first], 2))

    rows = ordered(xl, ordered(c, column, core), ordered(c, across, both))
    return rows.reshape(kinds, 8, 256, cols)


def shards(tokens, weights, landmark_pos):
    tok_rows = tokens.shape[0]
    heads_dev = landmark_pos.shape[0]
    head_cols = weights.shape[2]
    head_size = head_cols // heads_dev
    c = lax.axis_index("c")
    group = lax.axis_index(SEQ)
    whole = gather_tokens(tokens)
    column = lax.all_gather(weights, "z", axis=1, tiled=True).reshape(3, 16, 32, head_cols)
    column_qk, column_v = column[:2], column[2:]
    across_qk, core_qk = shift(column_qk, "xl", 1), shift(column_qk, "c", 1)
    across_qk, column_v = lax.optimization_barrier((across_qk, column_v))
    both_qk = shift(across_qk, "c", 1)
    across_v, core_v = shift(column_v, "xl", 1), shift(column_v, "c", 1)

    def project(matrix):
        flat = jnp.einsum("btd,kbdc->ktc", whole, matrix, preferred_element_type=jnp.float32)
        parts = flat.astype(jnp.bfloat16).reshape(-1, tok_rows, heads_dev, head_size)
        return jnp.transpose(parts, (0, 2, 1, 3))

    query, keys = project(in_order(column_qk, core_qk, across_qk, both_qk))
    per_group = landmark_pos.shape[1] // 64
    local_pos = lax.dynamic_slice_in_dim(landmark_pos, group * per_group, per_group, 1)
    offsets = local_pos - group * tok_rows
    picker = (offsets[:, :, None] == jnp.arange(tok_rows, dtype=jnp.int32)[None, None, :]).astype(
        jnp.bfloat16
    )
    picked_q = jnp.einsum("hjt,hte->hje", picker, query, preferred_element_type=jnp.float32)
    picked_k = jnp.einsum("hjt,hte->hje", picker, keys, preferred_element_type=jnp.float32)
    even = (jnp.arange(per_group) % 2 == 0)[None, :, None]
    local_marks = jnp.where(even, picked_q, picked_k).astype(jnp.bfloat16)
    block = local_marks.reshape(heads_dev * per_group, head_size)
    spread = jnp.broadcast_to(block[None], (64,) + block.shape)
    spread, across_v = lax.optimization_barrier((spread, across_v))
    marks = lax.all_to_all(spread, SEQ, 0, 0, tiled=True)
    both_v = shift(across_v, "c", 1)
    values = project(in_order(column_v, core_v, across_v, both_v))[0]
    marks, values = lax.optimization_barrier((marks, values))
    landmarks = jnp.transpose(
        marks.reshape(64, heads_dev, per_group, head_size), (1, 0, 2, 3)
    ).reshape(heads_dev, 64 * per_group, head_size)
    key_weights = gauss(keys, landmarks).astype(jnp.bfloat16)
    partial = jnp.einsum("hte,htj->hej", values, key_weights, preferred_element_type=jnp.float32)
    give = lax.dynamic_index_in_dim(partial, 1 - c, 0, keepdims=False)
    keep = lax.dynamic_index_in_dim(partial, c, 0, keepdims=False)
    mine = lax.dynamic_index_in_dim(landmarks, c, 0, keepdims=True)
    chip = keep + shift(give, "c", 1)
    chip, mine = lax.optimization_barrier((chip, mine))
    iterate = invert(mine[0])
    pieces = lax.all_to_all(chip.reshape(32, -1, chip.shape[1]), ("z", "xl"), 0, 0, tiled=True)
    summed = jnp.sum(pieces, 0)
    mixed = lax.dot_general(
        summed, iterate, (((1,), (1,)), ((), ())), precision=lax.Precision.HIGHEST
    ).astype(jnp.bfloat16)
    one = lax.all_to_all(
        jnp.broadcast_to(mixed[None], (32,) + mixed.shape), ("z", "xl"), 0, 0, tiled=True
    ).reshape(head_size, -1)
    two = shift(one, "c", 1)
    mixed_all = jnp.where(c == 0, jnp.stack([one, two]), jnp.stack([two, one]))
    query_weights = gauss(query, landmarks).astype(jnp.bfloat16)
    result = jnp.einsum(
        "htm,hem->the", query_weights, mixed_all, preferred_element_type=jnp.float32
    )
    return result.reshape(tok_rows, head_cols).astype(jnp.bfloat16)


def solution(mesh):
    fine = Mesh(mesh.devices.reshape(SIZES), AXES)
    return jax.shard_map(
        shards,
        mesh=fine,
        in_specs=(P(SEQ, HEAD), P(None, SEQ, HEAD), P(HEAD, None)),
        out_specs=P(SEQ, HEAD),
        check_vma=False,
    )
```

```python
import math

import jax
import jax.numpy as jnp
from jax import lax
from jax.experimental import pallas as pl
from jax.experimental.pallas import tpu as pltpu
from jax.sharding import Mesh
from jax.sharding import PartitionSpec as P

NSTEPS = 6
AXES = ("y", "xh", "z", "xl", "c")
SIZES = (4, 2, 16, 2, 2)
HEAD = ("y", "xh")
SEQ = ("z", "xl", "c")
CHIPS = ("z", "xl")

VMEM = pl.BlockSpec(memory_space=pltpu.VMEM)
SMEM = pl.BlockSpec(memory_space=pltpu.SMEM)
ANY = pl.BlockSpec(memory_space=pltpu.HBM)
BF16 = jnp.bfloat16
F32 = jnp.float32
ROWS = (((1,), (1,)), ((), ()))
COLS = (((0,), (0,)), ((), ()))


def call(kernel, name, outs, ins, flops, nbytes, scratch=(), exps=0):
    return pl.pallas_call(
        kernel,
        out_shape=outs,
        in_specs=ins,
        out_specs=jax.tree.map(lambda _: VMEM, outs),
        scratch_shapes=list(scratch),
        cost_estimate=pl.CostEstimate(flops=flops, bytes_accessed=nbytes, transcendentals=exps),
        compiler_params=pltpu.CompilerParams(vmem_limit_bytes=16 << 20),
        name=name,
    )


def shift(value, axis, step):
    size = lax.axis_size(axis)
    return lax.ppermute(value, axis, [(i, (i + step) % size) for i in range(size)])


def high(left, right, dims=(((1,), (0,)), ((), ()))):
    return lax.dot_general(
        left, right, dims, precision=lax.Precision.HIGHEST, preferred_element_type=F32
    )


def side_norm(rows):
    rows32 = rows.astype(F32)
    ones = jnp.ones((8, rows.shape[1]), F32)
    return high(ones, rows32 * rows32, ROWS)[:1]


def down_norm(rows):
    rows32 = rows.astype(F32)
    return jnp.sum(rows32 * rows32, 1, keepdims=True)


def gauss(left, right, left_norm, right_norm):
    product = lax.dot_general(left, right, ROWS, preferred_element_type=F32)
    return jnp.exp((left_norm + right_norm - 2.0 * product) * (-0.5 / math.sqrt(left.shape[1])))


def load(kinds, first, tokens, pieces, x, w, sems):
    xl, c = lax.axis_index("xl"), lax.axis_index("c")
    places = ((xl, c), (xl, 1 - c), (1 - xl, c), (1 - xl, 1 - c))
    copies = []
    for piece, (row, core) in zip(pieces, places, strict=True):
        copies.append(
            pltpu.make_async_copy(
                piece.at[pl.ds(first, kinds)], w.at[:, :, row, core], sems.at[len(copies)]
            )
        )
    width = tokens.shape[2]
    for block in range(tokens.shape[0]):
        copies.append(
            pltpu.make_async_copy(
                tokens.at[block], x.at[:, pl.ds(block * width, width)], sems.at[len(copies)]
            )
        )
    for copy in copies:
        copy.start()
    for copy in copies:
        copy.wait()


def query_key_kernel(
    pos_ref, tokens, column, core, across, both, query, keys, spread, x, w, full, block, sems
):
    rows = x.shape[0]
    load(2, 0, tokens, (column, core, across, both), x, w, sems)
    depth = x.shape[1]

    @pl.loop(0, 3)
    def _(step):
        here = pl.ds(pl.multiple_of(step * (rows // 3), rows // 3), rows // 3)
        left = x[here, :]
        for kind, out in ((0, query), (1, keys)):
            flat = jnp.dot(left, w[kind].reshape(depth, -1), preferred_element_type=F32)
            for head in range(2):
                full[kind * 2 + head, here, :] = flat[:, head * 128 : (head + 1) * 128]
            out[here, :] = flat.astype(BF16)

    group = (lax.axis_index("z") * 2 + lax.axis_index("xl")) * 2 + lax.axis_index("c")
    for head in range(2):
        for mark in range(4):
            row = pos_ref[head, group * 4 + mark] - group * rows
            block[pl.ds(head * 4 + mark, 1), :] = full[(mark % 2) * 2 + head, pl.ds(row, 1), :]
    chosen = block[...].astype(BF16)
    for place in range(spread.shape[0]):
        spread[place] = chosen


def value_kernel(tokens, column, core, across, both, keys, values, norms, x, w, sems):
    rows, depth = x.shape
    load(1, 2, tokens, (column, core, across, both), x, w, sems)

    @pl.loop(0, 3)
    def _(step):
        here = pl.ds(pl.multiple_of(step * (rows // 3), rows // 3), rows // 3)
        flat = jnp.dot(x[here, :], w[0].reshape(depth, -1), preferred_element_type=F32)
        values[here, :] = flat.astype(BF16)
        for head in range(2):
            norms[head, here, :] = down_norm(keys[here, pl.ds(head * 128, 128)])


def summary_kernel(own, other, keys, values, norms, marks, give, keep, flat, part):
    c = lax.axis_index("c")
    flat[c] = own[...].reshape(256, 128).astype(F32)
    flat[1 - c] = other[...].reshape(256, 128).astype(F32)
    for head in range(2):
        pieces = [
            flat[core, pl.ds(head * 4 + mark, 32, stride=8), :]
            for core in range(2)
            for mark in range(4)
        ]
        marks[head] = jnp.concatenate(pieces, 0).astype(BF16)

    for head in range(2):
        rows = marks[head]
        cols = pl.ds(head * 128, 128)
        weights = gauss(keys[:, cols], rows, norms[head], side_norm(rows)).astype(BF16)
        part[head] = lax.dot_general(values[:, cols], weights, COLS, preferred_element_type=F32)

    for out, head in ((give, 1 - c), (keep, c)):
        for half in range(2):
            for four in range(4):
                out[pl.ds(half * 4 + four, 32, stride=8), :] = part[
                    head, pl.ds(four * 32, 32), pl.ds(half * 128, 128)
                ]


def inverse_kernel(marks_ref, inverse_ref):
    marks = marks_ref[lax.axis_index("c")]
    inner = gauss(marks, marks, down_norm(marks), side_norm(marks))
    scale_cols = jnp.max(jnp.sum(jnp.abs(inner), 0, keepdims=True), 1, keepdims=True)
    scale_rows = jnp.max(jnp.sum(jnp.abs(inner), 1, keepdims=True), 0, keepdims=True)
    iterate = inner / (scale_cols * scale_rows)
    for step in range(NSTEPS):
        iterate = 2.0 * iterate - high(high(iterate, inner), iterate)
    inverse_ref[...] = iterate


def mixed_kernel(pieces, inverse, spread):
    summed = jnp.sum(pieces[...], 0)
    left = high(summed, inverse[:, :128], ROWS)
    right = high(summed, inverse[:, 128:], ROWS)
    mixed = left[:4] + right[4:]
    chosen = jnp.concatenate([mixed[:, :128], mixed[:, 128:]], 0).astype(BF16)
    for place in range(spread.shape[0]):
        spread[place] = chosen


def query_weight_kernel(query, marks, weights):
    for head in range(2):
        rows = marks[head]
        left = query[:, pl.ds(head * 128, 128)]
        weights[head] = gauss(left, rows, down_norm(left), side_norm(rows)).astype(BF16)


def output_kernel(own, other, weights, out, flat):
    c = lax.axis_index("c")
    flat[c] = own[...].reshape(256, 128).astype(F32)
    flat[1 - c] = other[...].reshape(256, 128).astype(F32)
    for head in range(2):
        halves = [
            jnp.concatenate(
                [flat[head, pl.ds(half * 4 + four, 32, stride=8), :] for four in range(4)], 0
            )
            for half in range(2)
        ]
        mixed = jnp.concatenate(halves, 1).astype(BF16)
        out[:, pl.ds(head * 128, 128)] = lax.dot_general(
            weights[head], mixed, ROWS, preferred_element_type=F32
        ).astype(BF16)


def shape(dims, dtype):
    return jax.ShapeDtypeStruct(dims, dtype)


def shards(tokens, weights, landmark_pos):
    whole = lax.all_to_all(
        jnp.broadcast_to(tokens[None], (8,) + tokens.shape), HEAD, 0, 0, tiled=True
    )
    column = lax.all_gather(weights, "z", axis=1, tiled=True).reshape(3, 16, 32, 256)
    across, core = shift(column, "xl", 1), shift(column, "c", 1)
    both = shift(across, "c", 1)
    whole, column, core, across, both = (
        pltpu.with_memory_space_constraint(value, pltpu.HBM)
        for value in (whole, column, core, across, both)
    )
    place = pltpu.VMEM((768, 2048), BF16)
    sems = pltpu.SemaphoreType.DMA((12,))
    query, keys, spread = call(
        query_key_kernel,
        "query_keys",
        (shape((768, 256), BF16), shape((768, 256), BF16), shape((32, 8, 128), BF16)),
        [SMEM] + [ANY] * 5,
        2 * 768 * 2048 * 512,
        5 << 20,
        [
            place,
            pltpu.VMEM((2, 16, 2, 2, 32, 256), BF16),
            pltpu.VMEM((4, 768, 128), F32),
            pltpu.VMEM((8, 128), F32),
            sems,
        ],
    )(landmark_pos, whole, column, core, across, both)
    own_marks = lax.all_to_all(spread, CHIPS, 0, 0, tiled=True)
    values, norms = call(
        value_kernel,
        "values",
        (shape((768, 256), BF16), shape((2, 768, 1), F32)),
        [ANY] * 5 + [VMEM],
        2 * 768 * 2048 * 256,
        4 << 20,
        [place, pltpu.VMEM((1, 16, 2, 2, 32, 256), BF16), sems],
    )(whole, column, core, across, both, keys)
    own_marks, values = lax.optimization_barrier((own_marks, values))
    other_marks = shift(own_marks, "c", 1)
    marks, give, keep = call(
        summary_kernel,
        "summary",
        (shape((2, 256, 128), BF16), shape((256, 128), F32), shape((256, 128), F32)),
        [VMEM] * 5,
        2 * 2 * 2 * 768 * 256 * 128,
        2 << 20,
        [pltpu.VMEM((2, 256, 128), F32), pltpu.VMEM((2, 128, 256), F32)],
        2 * 768 * 256,
    )(own_marks, other_marks, keys, values, norms)
    chip = keep + shift(give, "c", 1)
    chip, marks = lax.optimization_barrier((chip, marks))
    inverse = call(
        inverse_kernel,
        "inverse",
        shape((256, 256), F32),
        [VMEM],
        2 * 6 * 12 * 256**3,
        1 << 19,
        (),
        256 * 256,
    )(marks)
    pieces = lax.all_to_all(chip.reshape(32, 8, 128), CHIPS, 0, 0, tiled=True)
    mixed = call(
        mixed_kernel,
        "mixed",
        shape((32, 8, 128), BF16),
        [VMEM] * 2,
        2 * 6 * 16 * 256 * 128,
        1 << 19,
    )(pieces, inverse)
    mixed, marks, query = lax.optimization_barrier((mixed, marks, query))
    own_mixed = lax.all_to_all(mixed, CHIPS, 0, 0, tiled=True)
    query_weights = call(
        query_weight_kernel,
        "query_weights",
        shape((2, 768, 256), BF16),
        [VMEM] * 2,
        2 * 2 * 768 * 256 * 128,
        2 << 20,
        (),
        2 * 768 * 256,
    )(query, marks)
    own_mixed, query_weights = lax.optimization_barrier((own_mixed, query_weights))
    other_mixed = shift(own_mixed, "c", 1)
    return call(
        output_kernel,
        "attended",
        shape((768, 256), BF16),
        [VMEM] * 3,
        2 * 2 * 768 * 256 * 128,
        2 << 20,
        [pltpu.VMEM((2, 256, 128), F32)],
    )(own_mixed, other_mixed, query_weights)


def solution(mesh):
    fine = Mesh(mesh.devices.reshape(SIZES), AXES)
    return jax.shard_map(
        shards,
        mesh=fine,
        in_specs=(P(SEQ, HEAD), P(None, SEQ, HEAD), P(HEAD, None)),
        out_specs=P(SEQ, HEAD),
        check_vma=False,
    )
```

```python
import math

import jax
import jax.numpy as jnp
from jax import lax
from jax.experimental import pallas as pl
from jax.experimental.pallas import tpu as pltpu
from jax.sharding import Mesh
from jax.sharding import PartitionSpec as P

NSTEPS = 6
AXES = ("y", "xh", "z", "xl", "c")
SIZES = (4, 2, 16, 2, 2)
HEAD = ("y", "xh")
SEQ = ("z", "xl", "c")
CHIPS = ("z", "xl")

VMEM = pl.BlockSpec(memory_space=pltpu.VMEM)
SMEM = pl.BlockSpec(memory_space=pltpu.SMEM)
HBM = pl.BlockSpec(memory_space=pltpu.HBM)
ANY = pl.BlockSpec(memory_space=pl.ANY)
BF16 = jnp.bfloat16
F32 = jnp.float32
ROWS = (((1,), (1,)), ((), ()))
COLS = (((0,), (0,)), ((), ()))


def call(kernel, name, outs, ins, flops, nbytes, scratch=(), exps=0):
    return pl.pallas_call(
        kernel,
        out_shape=outs,
        in_specs=ins,
        out_specs=jax.tree.map(lambda _: VMEM, outs),
        scratch_shapes=list(scratch),
        cost_estimate=pl.CostEstimate(flops=flops, bytes_accessed=nbytes, transcendentals=exps),
        compiler_params=pltpu.CompilerParams(vmem_limit_bytes=16 << 20),
        name=name,
    )


def shift(value, axis, step):
    size = lax.axis_size(axis)
    return lax.ppermute(value, axis, [(i, (i + step) % size) for i in range(size)])


def high(left, right, dims=(((1,), (0,)), ((), ()))):
    return lax.dot_general(
        left, right, dims, precision=lax.Precision.HIGHEST, preferred_element_type=F32
    )


def side_norm(rows):
    rows32 = rows.astype(F32)
    ones = jnp.ones((8, rows.shape[1]), F32)
    return high(ones, rows32 * rows32, ROWS)[:1]


def down_norm(rows):
    rows32 = rows.astype(F32)
    return jnp.sum(rows32 * rows32, 1, keepdims=True)


def gauss(left, right, left_norm, right_norm):
    product = lax.dot_general(left, right, ROWS, preferred_element_type=F32)
    return jnp.exp((left_norm + right_norm - 2.0 * product) * (-0.5 / math.sqrt(left.shape[1])))


def run(copies):
    for copy in copies:
        copy.start()
    for copy in copies:
        copy.wait()


def pick_kernel(pos_ref, tokens, picked, groups, rows, sems):
    group = (lax.axis_index("z") * 2 + lax.axis_index("xl")) * 2 + lax.axis_index("c")
    blocks, count, width = tokens.shape
    places, copies = [], []
    for mark in range(8):
        row = pos_ref[mark // 4, group * 4 + mark % 4] - group * count
        start = pl.multiple_of((row // 8) * 8, 8)
        places.append(row - start)
        copies.append(
            pltpu.make_async_copy(
                tokens.at[:, pl.ds(start, 8), :], groups.at[mark], sems.at[mark]
            )
        )
    run(copies)
    index = lax.broadcasted_iota(jnp.int32, (8, width), 0)
    for mark, place in enumerate(places):
        for block in range(blocks):
            eight = groups[mark, block].astype(F32)
            rows[pl.ds(mark, 1), pl.ds(block * width, width)] = jnp.sum(
                jnp.where(index == place, eight, 0.0), 0, keepdims=True
            )
    picked[...] = rows[...].astype(BF16)


def partial_kernel(own, other, column, core, keep, give, w, sems):
    xl, c = lax.axis_index("xl"), lax.axis_index("c")
    run(
        [
            pltpu.make_async_copy(column.at[pl.ds(0, 2)], w.at[:, :, c], sems.at[0]),
            pltpu.make_async_copy(core.at[pl.ds(0, 2)], w.at[:, :, 1 - c], sems.at[1]),
        ]
    )
    rows = jnp.concatenate([own[...].astype(F32), other[...].astype(F32)], 0)
    low = lax.broadcasted_iota(jnp.int32, (16, 128), 1) < 64
    tiles = []
    for pair in range(8):
        even = rows[:, pair * 256 : pair * 256 + 128]
        odd = rows[:, pair * 256 + 128 : pair * 256 + 256]
        first = jnp.where(low, even, pltpu.roll(odd, 64, 1))
        second = jnp.where(low, pltpu.roll(even, 64, 1), odd)
        tiles.append(jnp.where(xl == 0, first, second))
    left = jnp.concatenate(tiles, 1).astype(BF16)
    results = [
        jnp.dot(left, w[kind].reshape(1024, 256), preferred_element_type=F32) for kind in range(2)
    ]
    number = lax.broadcasted_iota(jnp.int32, (16, 256), 0)
    both = jnp.where(number % 2 == 0, results[0], results[1])
    chosen = jnp.where((number[:, :128] % 8) < 4, both[:, :128], both[:, 128:])
    keep[...] = chosen[:8]
    give[...] = chosen[8:]


def finish_kernel(keep, received, spread):
    chosen = (keep[...] + received[...]).astype(BF16)
    for place in range(spread.shape[0]):
        spread[place] = chosen


def project_kernel(
    tokens, column, core, across, both, query, keys, values, norms, x, w, sems
):
    rows, depth = x.shape
    xl, c = lax.axis_index("xl"), lax.axis_index("c")
    places = (
        (column, xl, c), (core, xl, 1 - c), (across, 1 - xl, c), (both, 1 - xl, 1 - c)
    )
    copies = [
        pltpu.make_async_copy(piece, w.at[:, :, row, part], sems.at[number])
        for number, (piece, row, part) in enumerate(places)
    ]
    width = tokens.shape[2]
    for block in range(tokens.shape[0]):
        copies.append(
            pltpu.make_async_copy(
                tokens.at[block], x.at[:, pl.ds(block * width, width)], sems.at[4 + block]
            )
        )
    run(copies)

    @pl.loop(0, 3)
    def _(step):
        here = pl.ds(pl.multiple_of(step * (rows // 3), rows // 3), rows // 3)
        left = x[here, :]
        for kind, out in ((0, query), (1, keys), (2, values)):
            out[here, :] = jnp.dot(
                left, w[kind].reshape(depth, -1), preferred_element_type=F32
            ).astype(BF16)
        for head in range(2):
            norms[head, here, :] = down_norm(keys[here, pl.ds(head * 128, 128)])


def summary_kernel(own, other, keys, values, norms, marks, give, keep, flat, part):
    c = lax.axis_index("c")
    flat[c] = own[...].reshape(256, 128).astype(F32)
    flat[1 - c] = other[...].reshape(256, 128).astype(F32)
    for head in range(2):
        pieces = [
            flat[core, pl.ds(head * 4 + mark, 32, stride=8), :]
            for core in range(2)
            for mark in range(4)
        ]
        marks[head] = jnp.concatenate(pieces, 0).astype(BF16)

    for head in range(2):
        rows = marks[head]
        cols = pl.ds(head * 128, 128)
        weights = gauss(keys[:, cols], rows, norms[head], side_norm(rows)).astype(BF16)
        part[head] = lax.dot_general(values[:, cols], weights, COLS, preferred_element_type=F32)

    for out, head in ((give, 1 - c), (keep, c)):
        for half in range(2):
            for four in range(4):
                out[pl.ds(half * 4 + four, 32, stride=8), :] = part[
                    head, pl.ds(four * 32, 32), pl.ds(half * 128, 128)
                ]


def inverse_kernel(marks_ref, inverse_ref):
    marks = marks_ref[lax.axis_index("c")]
    inner = gauss(marks, marks, down_norm(marks), side_norm(marks))
    scale_cols = jnp.max(jnp.sum(jnp.abs(inner), 0, keepdims=True), 1, keepdims=True)
    scale_rows = jnp.max(jnp.sum(jnp.abs(inner), 1, keepdims=True), 0, keepdims=True)
    iterate = inner / (scale_cols * scale_rows)
    for step in range(NSTEPS):
        iterate = 2.0 * iterate - high(high(iterate, inner), iterate)
    inverse_ref[...] = iterate


def mixed_kernel(pieces, inverse, spread):
    summed = jnp.sum(pieces[...], 0)
    left = high(summed, inverse[:, :128], ROWS)
    right = high(summed, inverse[:, 128:], ROWS)
    mixed = left[:4] + right[4:]
    chosen = jnp.concatenate([mixed[:, :128], mixed[:, 128:]], 0).astype(BF16)
    for place in range(spread.shape[0]):
        spread[place] = chosen


def query_weight_kernel(query, marks, weights):
    for head in range(2):
        rows = marks[head]
        left = query[:, pl.ds(head * 128, 128)]
        weights[head] = gauss(left, rows, down_norm(left), side_norm(rows)).astype(BF16)


def output_kernel(own, other, weights, out, flat):
    c = lax.axis_index("c")
    flat[c] = own[...].reshape(256, 128).astype(F32)
    flat[1 - c] = other[...].reshape(256, 128).astype(F32)
    for head in range(2):
        halves = [
            jnp.concatenate(
                [flat[head, pl.ds(half * 4 + four, 32, stride=8), :] for four in range(4)], 0
            )
            for half in range(2)
        ]
        mixed = jnp.concatenate(halves, 1).astype(BF16)
        out[:, pl.ds(head * 128, 128)] = lax.dot_general(
            weights[head], mixed, ROWS, preferred_element_type=F32
        ).astype(BF16)


def shape(dims, dtype):
    return jax.ShapeDtypeStruct(dims, dtype)


def shards(tokens, weights, landmark_pos):
    whole = lax.all_to_all(
        jnp.broadcast_to(tokens[None], (8,) + tokens.shape), HEAD, 0, 0, tiled=True
    )
    column = lax.all_gather(weights, "z", axis=1, tiled=True).reshape(3, 16, 32, 256)
    across, core = shift(column, "xl", 1), shift(column, "c", 1)
    column, core = (
        pltpu.with_memory_space_constraint(value, pltpu.HBM) for value in (column, core)
    )
    picked = call(
        pick_kernel,
        "pick",
        shape((8, 2048), BF16),
        [SMEM, ANY],
        1 << 20,
        1 << 19,
        [
            pltpu.VMEM((8, 8, 8, 256), BF16),
            pltpu.VMEM((8, 2048), F32),
            pltpu.SemaphoreType.DMA((8,)),
        ],
    )(landmark_pos, whole)
    other_picked = shift(picked, "xl", 1)
    keep, give = call(
        partial_kernel,
        "partial",
        (shape((8, 128), F32), shape((8, 128), F32)),
        [VMEM, VMEM, HBM, HBM],
        2 * 16 * 1024 * 512,
        1 << 20,
        [pltpu.VMEM((2, 16, 2, 32, 256), BF16), pltpu.SemaphoreType.DMA((2,))],
    )(picked, other_picked, column, core)
    received = shift(give, "xl", 1)
    spread = call(
        finish_kernel, "finish", shape((32, 8, 128), BF16), [VMEM] * 2, 1 << 14, 1 << 16
    )(keep, received)
    own_marks = lax.all_to_all(spread, CHIPS, 0, 0, tiled=True)
    across, spread = lax.optimization_barrier((across, spread))
    both = shift(across, "c", 1)
    across, both = (
        pltpu.with_memory_space_constraint(value, pltpu.HBM) for value in (across, both)
    )
    query, keys, values, norms = call(
        project_kernel,
        "project",
        (
            shape((768, 256), BF16),
            shape((768, 256), BF16),
            shape((768, 256), BF16),
            shape((2, 768, 1), F32),
        ),
        [ANY] + [HBM] * 4,
        1 << 16,
        1 << 16,
        [
            pltpu.VMEM((768, 2048), BF16),
            pltpu.VMEM((3, 16, 2, 2, 32, 256), BF16),
            pltpu.SemaphoreType.DMA((12,)),
        ],
    )(whole, column, core, across, both)
    own_marks, values = lax.optimization_barrier((own_marks, values))
    other_marks = shift(own_marks, "c", 1)
    marks, give, keep = call(
        summary_kernel,
        "summary",
        (shape((2, 256, 128), BF16), shape((256, 128), F32), shape((256, 128), F32)),
        [VMEM] * 5,
        2 * 2 * 2 * 768 * 256 * 128,
        2 << 20,
        [pltpu.VMEM((2, 256, 128), F32), pltpu.VMEM((2, 128, 256), F32)],
        2 * 768 * 256,
    )(own_marks, other_marks, keys, values, norms)
    chip = keep + shift(give, "c", 1)
    chip, marks = lax.optimization_barrier((chip, marks))
    inverse = call(
        inverse_kernel,
        "inverse",
        shape((256, 256), F32),
        [VMEM],
        2 * 6 * 12 * 256**3,
        1 << 19,
        (),
        256 * 256,
    )(marks)
    pieces = lax.all_to_all(chip.reshape(32, 8, 128), CHIPS, 0, 0, tiled=True)
    mixed = call(
        mixed_kernel,
        "mixed",
        shape((32, 8, 128), BF16),
        [VMEM] * 2,
        2 * 6 * 16 * 256 * 128,
        1 << 19,
    )(pieces, inverse)
    mixed, marks, query = lax.optimization_barrier((mixed, marks, query))
    own_mixed = lax.all_to_all(mixed, CHIPS, 0, 0, tiled=True)
    query_weights = call(
        query_weight_kernel,
        "query_weights",
        shape((2, 768, 256), BF16),
        [VMEM] * 2,
        2 * 2 * 768 * 256 * 128,
        2 << 20,
        (),
        2 * 768 * 256,
    )(query, marks)
    own_mixed, query_weights = lax.optimization_barrier((own_mixed, query_weights))
    other_mixed = shift(own_mixed, "c", 1)
    return call(
        output_kernel,
        "attended",
        shape((768, 256), BF16),
        [VMEM] * 3,
        2 * 2 * 768 * 256 * 128,
        2 << 20,
        [pltpu.VMEM((2, 256, 128), F32)],
    )(own_mixed, other_mixed, query_weights)


def solution(mesh):
    fine = Mesh(mesh.devices.reshape(SIZES), AXES)
    return jax.shard_map(
        shards,
        mesh=fine,
        in_specs=(P(SEQ, HEAD), P(None, SEQ, HEAD), P(HEAD, None)),
        out_specs=P(SEQ, HEAD),
        check_vma=False,
    )
```

```python
import math

import jax
import jax.numpy as jnp
from jax import lax
from jax.experimental import pallas as pl
from jax.experimental.pallas import tpu as pltpu
from jax.sharding import Mesh
from jax.sharding import PartitionSpec as P

NSTEPS = 6
AXES = ("y", "xh", "z", "xl", "c")
SIZES = (4, 2, 16, 2, 2)
HEAD = ("y", "xh")
SEQ = ("z", "xl", "c")
CHIPS = ("z", "xl")
CORES = ("z", "c")

VMEM = pl.BlockSpec(memory_space=pltpu.VMEM)
SMEM = pl.BlockSpec(memory_space=pltpu.SMEM)
HBM = pl.BlockSpec(memory_space=pltpu.HBM)
ANY = pl.BlockSpec(memory_space=pl.ANY)
BF16 = jnp.bfloat16
F32 = jnp.float32
ROWS = (((1,), (1,)), ((), ()))
COLS = (((0,), (0,)), ((), ()))


def call(kernel, name, outs, ins, flops, nbytes, scratch=(), exps=0, space=VMEM):
    return pl.pallas_call(
        kernel,
        out_shape=outs,
        in_specs=ins,
        out_specs=jax.tree.map(lambda _: space, outs),
        scratch_shapes=list(scratch),
        cost_estimate=pl.CostEstimate(flops=flops, bytes_accessed=nbytes, transcendentals=exps),
        compiler_params=pltpu.CompilerParams(vmem_limit_bytes=16 << 20),
        name=name,
    )


def shift(value, axis, step):
    size = lax.axis_size(axis)
    return lax.ppermute(value, axis, [(i, (i + step) % size) for i in range(size)])


def high(left, right, dims=(((1,), (0,)), ((), ()))):
    return lax.dot_general(
        left, right, dims, precision=lax.Precision.HIGHEST, preferred_element_type=F32
    )


def side_norm(rows):
    rows32 = rows.astype(F32)
    ones = jnp.ones((8, rows.shape[1]), F32)
    return high(ones, rows32 * rows32, ROWS)[:1]


def down_norm(rows):
    rows32 = rows.astype(F32)
    return jnp.sum(rows32 * rows32, 1, keepdims=True)


def gauss(left, right, left_norm, right_norm):
    product = lax.dot_general(left, right, ROWS, preferred_element_type=F32)
    return jnp.exp((left_norm + right_norm - 2.0 * product) * (-0.5 / math.sqrt(left.shape[1])))


def run(copies):
    for copy in copies:
        copy.start()
    for copy in copies:
        copy.wait()


def pick_kernel(pos_ref, tokens, picked, groups, rows, sems):
    group = (lax.axis_index("z") * 2 + lax.axis_index("xl")) * 2 + lax.axis_index("c")
    blocks, count, width = tokens.shape
    places, copies = [], []
    for mark in range(8):
        row = pos_ref[mark // 4, group * 4 + mark % 4] - group * count
        start = pl.multiple_of((row // 8) * 8, 8)
        places.append(row - start)
        copies.append(
            pltpu.make_async_copy(
                tokens.at[:, pl.ds(start, 8), :], groups.at[mark], sems.at[mark]
            )
        )
    run(copies)
    index = lax.broadcasted_iota(jnp.int32, (8, width), 0)
    for mark, place in enumerate(places):
        for block in range(blocks):
            eight = groups[mark, block].astype(F32)
            rows[pl.ds(mark, 1), pl.ds(block * width, width)] = jnp.sum(
                jnp.where(index == place, eight, 0.0), 0, keepdims=True
            )
    picked[...] = rows[...].astype(BF16)


def partial_kernel(own, other, column, core, keep, give, w, sems):
    xl, c = lax.axis_index("xl"), lax.axis_index("c")
    run(
        [
            pltpu.make_async_copy(column.at[pl.ds(0, 2)], w.at[:, :, c], sems.at[0]),
            pltpu.make_async_copy(core.at[pl.ds(0, 2)], w.at[:, :, 1 - c], sems.at[1]),
        ]
    )
    rows = jnp.concatenate([own[...].astype(F32), other[...].astype(F32)], 0)
    low = lax.broadcasted_iota(jnp.int32, (16, 128), 1) < 64
    tiles = []
    for pair in range(8):
        even = rows[:, pair * 256 : pair * 256 + 128]
        odd = rows[:, pair * 256 + 128 : pair * 256 + 256]
        first = jnp.where(low, even, pltpu.roll(odd, 64, 1))
        second = jnp.where(low, pltpu.roll(even, 64, 1), odd)
        tiles.append(jnp.where(xl == 0, first, second))
    left = jnp.concatenate(tiles, 1).astype(BF16)
    results = [
        jnp.dot(left, w[kind].reshape(1024, 256), preferred_element_type=F32) for kind in range(2)
    ]
    number = lax.broadcasted_iota(jnp.int32, (16, 256), 0)
    both = jnp.where(number % 2 == 0, results[0], results[1])
    chosen = jnp.where((number[:, :128] % 8) < 4, both[:, :128], both[:, 128:])
    keep[...] = chosen[:8]
    give[...] = chosen[8:]


def finish_kernel(keep, received, spread):
    chosen = (keep[...] + received[...]).astype(BF16)
    for place in range(spread.shape[0]):
        spread[place] = chosen


def pack_kernel(column, core, packed, sems):
    c = lax.axis_index("c")
    cols = pl.ds(pl.multiple_of(c * 128, 128), 128)
    run(
        [
            pltpu.make_async_copy(column.at[:, :, :, cols], packed.at[c], sems.at[0]),
            pltpu.make_async_copy(core.at[:, :, :, cols], packed.at[1 - c], sems.at[1]),
        ]
    )


def project_kernel(tokens, core_tokens, packed, across, query, keys, values, norms, x, w, sems):
    depth = x.shape[1]
    xl = lax.axis_index("xl")
    copies = []

    def add(source, target):
        copies.append(pltpu.make_async_copy(source, target, sems.at[len(copies)]))

    for part in range(2):
        add(packed.at[part], w.at[:, :, xl, part])
        add(across.at[part], w.at[:, :, 1 - xl, part])
    blocks, rows, width = tokens.shape
    for number, source in enumerate((tokens, core_tokens)):
        for block in range(blocks):
            add(
                source.at[block],
                x.at[pl.ds(number * rows, rows), pl.ds(block * width, width)],
            )
    run(copies)
    weights = [w[kind].reshape(depth, 128) for kind in range(3)]
    pair = jnp.concatenate(weights[:2], 1)

    @pl.loop(0, 6)
    def _(step):
        here = pl.ds(pl.multiple_of(step * 256, 256), 256)
        left = x[here, :]
        both = jnp.dot(left, pair, preferred_element_type=F32).astype(BF16)
        query[here, :] = both[:, :128]
        keys[here, :] = both[:, 128:]
        values[here, :] = jnp.dot(left, weights[2], preferred_element_type=F32).astype(BF16)
        norms[here, :] = down_norm(both[:, 128:])


def summary_kernel(own, other, keys, values, norms, marks, pieces, flat, part):
    xl, c = lax.axis_index("xl"), lax.axis_index("c")
    flat[xl] = own[...].reshape(256, 128).astype(F32)
    flat[1 - xl] = other[...].reshape(256, 128).astype(F32)
    rows = []
    for side in range(2):
        for mark in range(4):
            first = flat[side, pl.ds(mark, 32, stride=8), :]
            second = flat[side, pl.ds(4 + mark, 32, stride=8), :]
            rows.append(jnp.where(c == 0, first, second))
    rows = jnp.concatenate(rows, 0).astype(BF16)
    marks[...] = rows
    weights = gauss(keys[...], rows, norms[...], side_norm(rows)).astype(BF16)
    part[...] = lax.dot_general(values[...], weights, COLS, preferred_element_type=F32)
    for half in range(2):
        for four in range(4):
            pieces[pl.ds(half * 4 + four, 32, stride=8), :] = part[
                pl.ds(four * 32, 32), pl.ds(half * 128, 128)
            ]


def inverse_kernel(marks_ref, inverse_ref):
    marks = marks_ref[...]
    inner = gauss(marks, marks, down_norm(marks), side_norm(marks))
    scale_cols = jnp.max(jnp.sum(jnp.abs(inner), 0, keepdims=True), 1, keepdims=True)
    scale_rows = jnp.max(jnp.sum(jnp.abs(inner), 1, keepdims=True), 0, keepdims=True)
    iterate = inner / (scale_cols * scale_rows)
    for step in range(NSTEPS):
        iterate = 2.0 * iterate - high(high(iterate, inner), iterate)
    inverse_ref[...] = iterate


def mixed_kernel(pieces, inverse, spread):
    summed = jnp.sum(pieces[...], 0)
    left = high(summed, inverse[:, :128], ROWS)
    right = high(summed, inverse[:, 128:], ROWS)
    mixed = left[:4] + right[4:]
    chosen = jnp.concatenate([mixed[:, :128], mixed[:, 128:]], 0).astype(BF16)
    for place in range(spread.shape[0]):
        spread[place] = chosen


def query_weight_kernel(query, marks, weights):
    rows = marks[...]
    weights[...] = gauss(query[...], rows, down_norm(query[...]), side_norm(rows)).astype(BF16)


def give_kernel(spread, weights, mixed, give, flat):
    flat[...] = spread[...].reshape(256, 128).astype(F32)
    halves = [
        jnp.concatenate([flat[pl.ds(half * 4 + four, 32, stride=8), :] for four in range(4)], 0)
        for half in range(2)
    ]
    matrix = jnp.concatenate(halves, 1).astype(BF16)
    mixed[...] = matrix
    give[...] = lax.dot_general(
        weights[768:, :], matrix, ROWS, preferred_element_type=F32
    ).astype(BF16)


def keep_kernel(mixed, weights, keep):
    keep[...] = lax.dot_general(
        weights[:768, :], mixed[...], ROWS, preferred_element_type=F32
    ).astype(BF16)


def join_kernel(keep, received, out):
    c = lax.axis_index("c")
    out[:, pl.ds(pl.multiple_of(c * 128, 128), 128)] = keep[...]
    out[:, pl.ds(pl.multiple_of((1 - c) * 128, 128), 128)] = received[...]


def shape(dims, dtype):
    return jax.ShapeDtypeStruct(dims, dtype)


def shards(tokens, weights, landmark_pos):
    whole = lax.all_to_all(
        jnp.broadcast_to(tokens[None], (8,) + tokens.shape), HEAD, 0, 0, tiled=True
    )
    column = lax.all_gather(weights, "z", axis=1, tiled=True).reshape(3, 16, 32, 256)
    core = shift(column, "c", 1)
    core, later = lax.optimization_barrier((core, whole))
    core_tokens = shift(later, "c", 1)
    packed = call(
        pack_kernel,
        "pack",
        shape((2, 3, 16, 32, 128), BF16),
        [ANY, ANY],
        1 << 10,
        3 << 19,
        [pltpu.SemaphoreType.DMA((2,))],
        space=HBM,
    )(column, core)
    picked = call(
        pick_kernel,
        "pick",
        shape((8, 2048), BF16),
        [SMEM, ANY],
        1 << 20,
        1 << 19,
        [
            pltpu.VMEM((8, 8, 8, 256), BF16),
            pltpu.VMEM((8, 2048), F32),
            pltpu.SemaphoreType.DMA((8,)),
        ],
    )(landmark_pos, whole)
    other_picked = shift(picked, "xl", 1)
    keep, give = call(
        partial_kernel,
        "partial",
        (shape((8, 128), F32), shape((8, 128), F32)),
        [VMEM, VMEM, ANY, ANY],
        2 * 16 * 1024 * 512,
        1 << 20,
        [pltpu.VMEM((2, 16, 2, 32, 256), BF16), pltpu.SemaphoreType.DMA((2,))],
    )(picked, other_picked, column, core)
    received = shift(give, "xl", 1)
    spread = call(
        finish_kernel, "finish", shape((32, 8, 128), BF16), [VMEM] * 2, 1 << 14, 1 << 16
    )(keep, received)
    spread, packed = lax.optimization_barrier((spread, packed))
    own_marks = lax.all_to_all(spread, CORES, 0, 0, tiled=True)
    across = shift(packed, "xl", 1)
    query, keys, values, norms = call(
        project_kernel,
        "project",
        (
            shape((1536, 128), BF16),
            shape((1536, 128), BF16),
            shape((1536, 128), BF16),
            shape((1536, 1), F32),
        ),
        [ANY] * 4,
        2 * 1536 * 2048 * 384,
        8 << 20,
        [
            pltpu.VMEM((1536, 2048), BF16),
            pltpu.VMEM((3, 16, 2, 2, 32, 128), BF16),
            pltpu.SemaphoreType.DMA((20,)),
        ],
    )(whole, core_tokens, packed, across)

    other_marks = shift(own_marks, "xl", 1)
    marks, chip = call(
        summary_kernel,
        "summary",
        (shape((256, 128), BF16), shape((256, 128), F32)),
        [VMEM] * 5,
        2 * 2 * 1536 * 256 * 128,
        2 << 20,
        [pltpu.VMEM((2, 256, 128), F32), pltpu.VMEM((128, 256), F32)],
        1536 * 256,
    )(own_marks, other_marks, keys, values, norms)
    chip, marks, query = lax.optimization_barrier((chip, marks, query))
    inverse = call(
        inverse_kernel,
        "inverse",
        shape((256, 256), F32),
        [VMEM],
        2 * 6 * 12 * 256**3,
        1 << 19,
        (),
        256 * 256,
    )(marks)
    query_weights = call(
        query_weight_kernel,
        "query_weights",
        shape((1536, 256), BF16),
        [VMEM] * 2,
        2 * 1536 * 256 * 128,
        2 << 20,
        (),
        1536 * 256,
    )(query, marks)
    pieces = lax.all_to_all(chip.reshape(32, 8, 128), CHIPS, 0, 0, tiled=True)
    pieces, query_weights = lax.optimization_barrier((pieces, query_weights))
    spread = call(
        mixed_kernel,
        "mixed",
        shape((32, 8, 128), BF16),
        [VMEM] * 2,
        2 * 6 * 16 * 256 * 128,
        1 << 19,
    )(pieces, inverse)
    spread = lax.all_to_all(spread, CHIPS, 0, 0, tiled=True)
    mixed, give = call(
        give_kernel,
        "give",
        (shape((128, 256), BF16), shape((768, 128), BF16)),
        [VMEM] * 2,
        2 * 768 * 256 * 128,
        1 << 19,
        [pltpu.VMEM((256, 128), F32)],
    )(spread, query_weights)
    received = shift(give, "c", 1)
    keep = call(
        keep_kernel,
        "keep",
        shape((768, 128), BF16),
        [VMEM] * 2,
        2 * 768 * 256 * 128,
        1 << 19,
    )(mixed, query_weights)
    return call(
        join_kernel, "join", shape((768, 256), BF16), [VMEM] * 2, 1 << 10, 1 << 19
    )(keep, received)


def solution(mesh):
    fine = Mesh(mesh.devices.reshape(SIZES), AXES)
    return jax.shard_map(
        shards,
        mesh=fine,
        in_specs=(P(SEQ, HEAD), P(None, SEQ, HEAD), P(HEAD, None)),
        out_specs=P(SEQ, HEAD),
        check_vma=False,
    )
```

```python
import math

import jax
import jax.numpy as jnp
from jax import lax
from jax.experimental import pallas as pl
from jax.experimental.pallas import tpu as pltpu
from jax.sharding import Mesh
from jax.sharding import PartitionSpec as P

NSTEPS = 6
AXES = ("y", "xh", "z", "xl", "c")
SIZES = (4, 2, 16, 2, 2)
HEAD = ("y", "xh")
SEQ = ("z", "xl", "c")
CHIPS = ("z", "xl")
CORES = ("z", "c")

VMEM = pl.BlockSpec(memory_space=pltpu.VMEM)
SMEM = pl.BlockSpec(memory_space=pltpu.SMEM)
HBM = pl.BlockSpec(memory_space=pltpu.HBM)
ANY = pl.BlockSpec(memory_space=pl.ANY)
BF16 = jnp.bfloat16
F32 = jnp.float32
ROWS = (((1,), (1,)), ((), ()))
COLS = (((0,), (0,)), ((), ()))


def call(kernel, name, outs, ins, flops, nbytes, scratch=(), exps=0, space=VMEM):
    return pl.pallas_call(
        kernel,
        out_shape=outs,
        in_specs=ins,
        out_specs=jax.tree.map(lambda _: space, outs),
        scratch_shapes=list(scratch),
        cost_estimate=pl.CostEstimate(flops=flops, bytes_accessed=nbytes, transcendentals=exps),
        compiler_params=pltpu.CompilerParams(vmem_limit_bytes=16 << 20),
        name=name,
    )


def shift(value, axis, step):
    size = lax.axis_size(axis)
    return lax.ppermute(value, axis, [(i, (i + step) % size) for i in range(size)])


def high(left, right, dims=(((1,), (0,)), ((), ()))):
    return lax.dot_general(
        left, right, dims, precision=lax.Precision.HIGHEST, preferred_element_type=F32
    )


def side_norm(rows):
    rows32 = rows.astype(F32)
    ones = jnp.ones((8, rows.shape[1]), F32)
    return high(ones, rows32 * rows32, ROWS)[:1]


def down_norm(rows):
    rows32 = rows.astype(F32)
    return jnp.sum(rows32 * rows32, 1, keepdims=True)


def gauss(left, right, left_norm, right_norm):
    product = lax.dot_general(left, right, ROWS, preferred_element_type=F32)
    return jnp.exp((left_norm + right_norm - 2.0 * product) * (-0.5 / math.sqrt(left.shape[1])))


def run(copies):
    for copy in copies:
        copy.start()
    for copy in copies:
        copy.wait()


def repeat_kernel(source, target, sems):
    run([pltpu.make_async_copy(source, target.at[i], sems.at[i]) for i in range(target.shape[0])])


def pick_kernel(pos_ref, tokens, picked, groups, rows, sems):
    group = (lax.axis_index("z") * 2 + lax.axis_index("xl")) * 2 + lax.axis_index("c")
    blocks, count, width = tokens.shape
    places, copies = [], []
    for mark in range(8):
        row = pos_ref[mark // 4, group * 4 + mark % 4] - group * count
        start = pl.multiple_of((row // 8) * 8, 8)
        places.append(row - start)
        copies.append(
            pltpu.make_async_copy(
                tokens.at[:, pl.ds(start, 8), :], groups.at[mark], sems.at[mark]
            )
        )
    run(copies)
    index = lax.broadcasted_iota(jnp.int32, (8, width), 0)
    for mark, place in enumerate(places):
        for block in range(blocks):
            eight = groups[mark, block].astype(F32)
            rows[pl.ds(mark, 1), pl.ds(block * width, width)] = jnp.sum(
                jnp.where(index == place, eight, 0.0), 0, keepdims=True
            )
    picked[...] = rows[...].astype(BF16)


def partial_kernel(own, other, column, core, keep, give, w, sems):
    xl, c = lax.axis_index("xl"), lax.axis_index("c")
    run(
        [
            pltpu.make_async_copy(column.at[pl.ds(0, 2)], w.at[:, :, c], sems.at[0]),
            pltpu.make_async_copy(core.at[pl.ds(0, 2)], w.at[:, :, 1 - c], sems.at[1]),
        ]
    )
    rows = jnp.concatenate([own[...].astype(F32), other[...].astype(F32)], 0)
    low = lax.broadcasted_iota(jnp.int32, (16, 128), 1) < 64
    tiles = []
    for pair in range(8):
        even = rows[:, pair * 256 : pair * 256 + 128]
        odd = rows[:, pair * 256 + 128 : pair * 256 + 256]
        first = jnp.where(low, even, pltpu.roll(odd, 64, 1))
        second = jnp.where(low, pltpu.roll(even, 64, 1), odd)
        tiles.append(jnp.where(xl == 0, first, second))
    left = jnp.concatenate(tiles, 1).astype(BF16)
    results = [
        jnp.dot(left, w[kind].reshape(1024, 256), preferred_element_type=F32) for kind in range(2)
    ]
    number = lax.broadcasted_iota(jnp.int32, (16, 256), 0)
    both = jnp.where(number % 2 == 0, results[0], results[1])
    chosen = jnp.where((number[:, :128] % 8) < 4, both[:, :128], both[:, 128:])
    keep[...] = chosen[:8]
    give[...] = chosen[8:]


def finish_kernel(keep, received, spread):
    chosen = (keep[...] + received[...]).astype(BF16)
    for place in range(spread.shape[0]):
        spread[place] = chosen


def pack_kernel(column, core, queries, pairs, sems):
    c = lax.axis_index("c")
    cols = pl.ds(pl.multiple_of(c * 128, 128), 128)
    copies = []
    for piece, part in ((column, c), (core, 1 - c)):
        for first, count, target in ((0, 1, queries), (1, 2, pairs)):
            copies.append(
                pltpu.make_async_copy(
                    piece.at[pl.ds(first, count), :, :, cols], target.at[part], sems.at[len(copies)]
                )
            )
    run(copies)


def fill(tokens, core_tokens, packed, across, x, w, sems):
    xl = lax.axis_index("xl")
    copies = []

    def add(source, target):
        copies.append(pltpu.make_async_copy(source, target, sems.at[len(copies)]))

    for part in range(2):
        add(packed.at[part], w.at[:, :, xl, part])
        add(across.at[part], w.at[:, :, 1 - xl, part])
    blocks, rows, width = tokens.shape
    for number, source in enumerate((tokens, core_tokens)):
        for block in range(blocks):
            add(
                source.at[block],
                x.at[pl.ds(number * rows, rows), pl.ds(block * width, width)],
            )
    run(copies)


def key_value_kernel(tokens, core_tokens, packed, across, keys, values, x, w, k, v, sems):
    fill(tokens, core_tokens, packed, across, x, w, sems)
    depth = x.shape[1]
    pair = jnp.concatenate([w[kind].reshape(depth, 128) for kind in range(2)], 1)

    @pl.loop(0, 6)
    def _(step):
        here = pl.ds(pl.multiple_of(step * 256, 256), 256)
        both = jnp.dot(x[here, :], pair, preferred_element_type=F32).astype(BF16)
        k[here, :] = both[:, :128]
        v[here, :] = both[:, 128:]

    run(
        [
            pltpu.make_async_copy(k, keys, sems.at[0]),
            pltpu.make_async_copy(v, values, sems.at[1]),
        ]
    )


def query_kernel(tokens, core_tokens, packed, across, query, x, w, sems):
    fill(tokens, core_tokens, packed, across, x, w, sems)
    matrix = w[0].reshape(x.shape[1], 128)

    @pl.loop(0, 6)
    def _(step):
        here = pl.ds(pl.multiple_of(step * 256, 256), 256)
        query[here, :] = jnp.dot(x[here, :], matrix, preferred_element_type=F32).astype(BF16)


def summary_kernel(own, other, keys_in, values_in, marks, pieces, flat, part, keys, values, sems):
    xl, c = lax.axis_index("xl"), lax.axis_index("c")
    copies = [
        pltpu.make_async_copy(keys_in, keys, sems.at[0]),
        pltpu.make_async_copy(values_in, values, sems.at[1]),
    ]
    for copy in copies:
        copy.start()
    flat[xl] = own[...].reshape(256, 128).astype(F32)
    flat[1 - xl] = other[...].reshape(256, 128).astype(F32)
    rows = []
    for side in range(2):
        for mark in range(4):
            first = flat[side, pl.ds(mark, 32, stride=8), :]
            second = flat[side, pl.ds(4 + mark, 32, stride=8), :]
            rows.append(jnp.where(c == 0, first, second))
    rows = jnp.concatenate(rows, 0).astype(BF16)
    marks[...] = rows
    for copy in copies:
        copy.wait()
    weights = gauss(keys[...], rows, down_norm(keys[...]), side_norm(rows)).astype(BF16)
    part[...] = lax.dot_general(values[...], weights, COLS, preferred_element_type=F32)
    for half in range(2):
        for four in range(4):
            pieces[pl.ds(half * 4 + four, 32, stride=8), :] = part[
                pl.ds(four * 32, 32), pl.ds(half * 128, 128)
            ]


def inverse_kernel(marks_ref, inverse_ref):
    marks = marks_ref[...]
    inner = gauss(marks, marks, down_norm(marks), side_norm(marks))
    scale_cols = jnp.max(jnp.sum(jnp.abs(inner), 0, keepdims=True), 1, keepdims=True)
    scale_rows = jnp.max(jnp.sum(jnp.abs(inner), 1, keepdims=True), 0, keepdims=True)
    iterate = inner / (scale_cols * scale_rows)
    for step in range(NSTEPS):
        iterate = 2.0 * iterate - high(high(iterate, inner), iterate)
    inverse_ref[...] = iterate


def mixed_kernel(pieces, inverse, spread):
    summed = jnp.sum(pieces[...], 0)
    left = high(summed, inverse[:, :128], ROWS)
    right = high(summed, inverse[:, 128:], ROWS)
    mixed = left[:4] + right[4:]
    chosen = jnp.concatenate([mixed[:, :128], mixed[:, 128:]], 0).astype(BF16)
    for place in range(spread.shape[0]):
        spread[place] = chosen


def query_weight_kernel(query, marks, weights):
    rows = marks[...]
    weights[...] = gauss(query[...], rows, down_norm(query[...]), side_norm(rows)).astype(BF16)


def give_kernel(spread, weights, mixed, give, flat):
    flat[...] = spread[...].reshape(256, 128).astype(F32)
    halves = [
        jnp.concatenate([flat[pl.ds(half * 4 + four, 32, stride=8), :] for four in range(4)], 0)
        for half in range(2)
    ]
    matrix = jnp.concatenate(halves, 1).astype(BF16)
    mixed[...] = matrix
    give[...] = lax.dot_general(
        weights[768:, :], matrix, ROWS, preferred_element_type=F32
    ).astype(BF16)


def keep_kernel(mixed, weights, keep):
    keep[...] = lax.dot_general(
        weights[:768, :], mixed[...], ROWS, preferred_element_type=F32
    ).astype(BF16)


def join_kernel(keep, received, out):
    c = lax.axis_index("c")
    out[:, pl.ds(pl.multiple_of(c * 128, 128), 128)] = keep[...]
    out[:, pl.ds(pl.multiple_of((1 - c) * 128, 128), 128)] = received[...]


def shape(dims, dtype):
    return jax.ShapeDtypeStruct(dims, dtype)


def in_hbm(*values):
    return tuple(pltpu.with_memory_space_constraint(value, pltpu.HBM) for value in values)


def shards(tokens, weights, landmark_pos):
    repeated = call(
        repeat_kernel,
        "repeat",
        shape((8, 768, 256), BF16),
        [VMEM],
        1 << 10,
        3 << 20,
        [pltpu.SemaphoreType.DMA((8,))],
        space=HBM,
    )(tokens)
    (repeated,) = in_hbm(repeated)
    whole = lax.all_to_all(repeated, HEAD, 0, 0, tiled=True)
    column = lax.all_gather(weights, "z", axis=1, tiled=True).reshape(3, 16, 32, 256)
    core = shift(column, "c", 1)
    column, core, whole = in_hbm(column, core, whole)
    picked = call(
        pick_kernel,
        "pick",
        shape((8, 2048), BF16),
        [SMEM, ANY],
        1 << 20,
        1 << 19,
        [
            pltpu.VMEM((8, 8, 8, 256), BF16),
            pltpu.VMEM((8, 2048), F32),
            pltpu.SemaphoreType.DMA((8,)),
        ],
    )(landmark_pos, whole)
    other_picked = shift(picked, "xl", 1)
    picked, core = lax.optimization_barrier((picked, core))
    packed_q, packed_kv = call(
        pack_kernel,
        "pack",
        (shape((2, 1, 16, 32, 128), BF16), shape((2, 2, 16, 32, 128), BF16)),
        [ANY, ANY],
        1 << 10,
        3 << 19,
        [pltpu.SemaphoreType.DMA((4,))],
        space=HBM,
    )(column, core)
    later, packed_q = lax.optimization_barrier((whole, packed_q))
    core_tokens = shift(later, "c", 1)
    keep, give = call(
        partial_kernel,
        "partial",
        (shape((8, 128), F32), shape((8, 128), F32)),
        [VMEM, VMEM, ANY, ANY],
        2 * 16 * 1024 * 512,
        1 << 20,
        [pltpu.VMEM((2, 16, 2, 32, 256), BF16), pltpu.SemaphoreType.DMA((2,))],
    )(picked, other_picked, column, core)
    received = shift(give, "xl", 1)
    spread = call(
        finish_kernel, "finish", shape((32, 8, 128), BF16), [VMEM] * 2, 1 << 14, 1 << 16
    )(keep, received)
    spread, packed_kv = lax.optimization_barrier((spread, packed_kv))
    own_marks = lax.all_to_all(spread, CORES, 0, 0, tiled=True)
    across_kv = shift(packed_kv, "xl", 1)
    across_kv, packed_q = lax.optimization_barrier((across_kv, packed_q))
    across_q = shift(packed_q, "xl", 1)
    everyone = pltpu.VMEM((1536, 2048), BF16)
    half = pltpu.VMEM((1536, 128), BF16)
    sems = pltpu.SemaphoreType.DMA((20,))
    keys, values = call(
        key_value_kernel,
        "key_values",
        (shape((1536, 128), BF16), shape((1536, 128), BF16)),
        [ANY] * 4,
        2 * 1536 * 2048 * 256,
        8 << 20,
        [everyone, pltpu.VMEM((2, 16, 2, 2, 32, 128), BF16), half, half, sems],
        space=HBM,
    )(whole, core_tokens, packed_kv, across_kv)
    keys, values = in_hbm(keys, values)
    own_marks, values = lax.optimization_barrier((own_marks, values))
    other_marks = shift(own_marks, "xl", 1)
    marks, chip = call(
        summary_kernel,
        "summary",
        (shape((256, 128), BF16), shape((256, 128), F32)),
        [VMEM, VMEM, HBM, HBM],
        2 * 2 * 1536 * 256 * 128,
        2 << 20,
        [
            pltpu.VMEM((2, 256, 128), F32),
            pltpu.VMEM((128, 256), F32),
            half,
            half,
            pltpu.SemaphoreType.DMA((2,)),
        ],
        1536 * 256,
    )(own_marks, other_marks, keys, values)
    packed_q, marks = lax.optimization_barrier((packed_q, marks))
    query = call(
        query_kernel,
        "queries",
        shape((1536, 128), BF16),
        [ANY] * 4,
        2 * 1536 * 2048 * 128,
        7 << 20,
        [everyone, pltpu.VMEM((1, 16, 2, 2, 32, 128), BF16), sems],
    )(whole, core_tokens, packed_q, across_q)
    inverse = call(
        inverse_kernel,
        "inverse",
        shape((256, 256), F32),
        [VMEM],
        2 * 6 * 12 * 256**3,
        1 << 19,
        (),
        256 * 256,
    )(marks)
    query_weights = call(
        query_weight_kernel,
        "query_weights",
        shape((1536, 256), BF16),
        [VMEM] * 2,
        2 * 1536 * 256 * 128,
        2 << 20,
        (),
        1536 * 256,
    )(query, marks)
    pieces = lax.all_to_all(chip.reshape(32, 8, 128), CHIPS, 0, 0, tiled=True)
    pieces, query_weights = lax.optimization_barrier((pieces, query_weights))
    spread = call(
        mixed_kernel,
        "mixed",
        shape((32, 8, 128), BF16),
        [VMEM] * 2,
        2 * 6 * 16 * 256 * 128,
        1 << 19,
    )(pieces, inverse)
    spread = lax.all_to_all(spread, CHIPS, 0, 0, tiled=True)
    mixed, give = call(
        give_kernel,
        "give",
        (shape((128, 256), BF16), shape((768, 128), BF16)),
        [VMEM] * 2,
        2 * 768 * 256 * 128,
        1 << 19,
        [pltpu.VMEM((256, 128), F32)],
    )(spread, query_weights)
    received = shift(give, "c", 1)
    keep = call(
        keep_kernel,
        "keep",
        shape((768, 128), BF16),
        [VMEM] * 2,
        2 * 768 * 256 * 128,
        1 << 19,
    )(mixed, query_weights)
    return call(
        join_kernel, "join", shape((768, 256), BF16), [VMEM] * 2, 1 << 10, 1 << 19
    )(keep, received)


def solution(mesh):
    fine = Mesh(mesh.devices.reshape(SIZES), AXES)
    return jax.shard_map(
        shards,
        mesh=fine,
        in_specs=(P(SEQ, HEAD), P(None, SEQ, HEAD), P(HEAD, None)),
        out_specs=P(SEQ, HEAD),
        check_vma=False,
    )
```

```python
import math

import jax
import jax.numpy as jnp
from jax import lax
from jax.experimental import pallas as pl
from jax.experimental.pallas import tpu as pltpu
from jax.sharding import Mesh
from jax.sharding import PartitionSpec as P

NSTEPS = 6
AXES = ("y", "xh", "z", "xl", "c")
SIZES = (4, 2, 16, 2, 2)
HEAD = ("y", "xh")
SEQ = ("z", "xl", "c")
CHIPS = ("z", "xl")
CORES = ("z", "c")

VMEM = pl.BlockSpec(memory_space=pltpu.VMEM)
SMEM = pl.BlockSpec(memory_space=pltpu.SMEM)
HBM = pl.BlockSpec(memory_space=pltpu.HBM)
ANY = pl.BlockSpec(memory_space=pl.ANY)
BF16 = jnp.bfloat16
F32 = jnp.float32
ROWS = (((1,), (1,)), ((), ()))
COLS = (((0,), (0,)), ((), ()))


def call(kernel, name, outs, ins, flops, nbytes, scratch=(), exps=0, space=VMEM):
    return pl.pallas_call(
        kernel,
        out_shape=outs,
        in_specs=ins,
        out_specs=jax.tree.map(lambda _: space, outs),
        scratch_shapes=list(scratch),
        cost_estimate=pl.CostEstimate(flops=flops, bytes_accessed=nbytes, transcendentals=exps),
        compiler_params=pltpu.CompilerParams(vmem_limit_bytes=16 << 20),
        name=name,
    )


def shift(value, axis, step):
    size = lax.axis_size(axis)
    return lax.ppermute(value, axis, [(i, (i + step) % size) for i in range(size)])


def high(left, right, dims=(((1,), (0,)), ((), ()))):
    return lax.dot_general(
        left, right, dims, precision=lax.Precision.HIGHEST, preferred_element_type=F32
    )


def side_norm(rows):
    rows32 = rows.astype(F32)
    ones = jnp.ones((8, rows.shape[1]), F32)
    return high(ones, rows32 * rows32, ROWS)[:1]


def down_norm(rows):
    rows32 = rows.astype(F32)
    return jnp.sum(rows32 * rows32, 1, keepdims=True)


def gauss(left, right, left_norm, right_norm):
    product = lax.dot_general(left, right, ROWS, preferred_element_type=F32)
    return jnp.exp((left_norm + right_norm - 2.0 * product) * (-0.5 / math.sqrt(left.shape[1])))


def run(copies):
    for copy in copies:
        copy.start()
    for copy in copies:
        copy.wait()


def pick_kernel(pos_ref, tokens, picked, groups, rows, sems):
    group = (lax.axis_index("z") * 2 + lax.axis_index("xl")) * 2 + lax.axis_index("c")
    blocks, count, width = tokens.shape
    places, copies = [], []
    for mark in range(8):
        row = pos_ref[mark // 4, group * 4 + mark % 4] - group * count
        start = pl.multiple_of((row // 8) * 8, 8)
        places.append(row - start)
        copies.append(
            pltpu.make_async_copy(
                tokens.at[:, pl.ds(start, 8), :], groups.at[mark], sems.at[mark]
            )
        )
    run(copies)
    index = lax.broadcasted_iota(jnp.int32, (8, width), 0)
    for mark, place in enumerate(places):
        for block in range(blocks):
            eight = groups[mark, block].astype(F32)
            rows[pl.ds(mark, 1), pl.ds(block * width, width)] = jnp.sum(
                jnp.where(index == place, eight, 0.0), 0, keepdims=True
            )
    picked[...] = rows[...].astype(BF16)


def partial_kernel(own, other, column, core, keep, give, w, sems):
    xl, c = lax.axis_index("xl"), lax.axis_index("c")
    run(
        [
            pltpu.make_async_copy(column.at[pl.ds(0, 2)], w.at[:, :, c], sems.at[0]),
            pltpu.make_async_copy(core.at[pl.ds(0, 2)], w.at[:, :, 1 - c], sems.at[1]),
        ]
    )
    rows = jnp.concatenate([own[...].astype(F32), other[...].astype(F32)], 0)
    low = lax.broadcasted_iota(jnp.int32, (16, 128), 1) < 64
    tiles = []
    for pair in range(8):
        even = rows[:, pair * 256 : pair * 256 + 128]
        odd = rows[:, pair * 256 + 128 : pair * 256 + 256]
        first = jnp.where(low, even, pltpu.roll(odd, 64, 1))
        second = jnp.where(low, pltpu.roll(even, 64, 1), odd)
        tiles.append(jnp.where(xl == 0, first, second))
    left = jnp.concatenate(tiles, 1).astype(BF16)
    results = [
        jnp.dot(left, w[kind].reshape(1024, 256), preferred_element_type=F32) for kind in range(2)
    ]
    number = lax.broadcasted_iota(jnp.int32, (16, 256), 0)
    both = jnp.where(number % 2 == 0, results[0], results[1])
    chosen = jnp.where((number[:, :128] % 8) < 4, both[:, :128], both[:, 128:])
    keep[...] = chosen[:8]
    give[...] = chosen[8:]


def finish_kernel(keep, received, spread):
    chosen = (keep[...] + received[...]).astype(BF16)
    for place in range(spread.shape[0]):
        spread[place] = chosen


def pack_kernel(column, core, packed, sems):
    c = lax.axis_index("c")
    cols = pl.ds(pl.multiple_of(c * 128, 128), 128)
    run(
        [
            pltpu.make_async_copy(column.at[:, :, :, cols], packed.at[c], sems.at[0]),
            pltpu.make_async_copy(core.at[:, :, :, cols], packed.at[1 - c], sems.at[1]),
        ]
    )


def project_kernel(tokens, core_tokens, packed, across, query, keys, values, norms, w, sems):
    xl = lax.axis_index("xl")
    copies = []
    for part in range(2):
        for source, row in ((packed, xl), (across, 1 - xl)):
            copies.append(
                pltpu.make_async_copy(
                    source.at[part], w.at[:, :, row, part], sems.at[len(copies)]
                )
            )
    run(copies)
    blocks, rows, width = tokens.shape
    weights = [w[kind].reshape(blocks * width, 128) for kind in range(3)]
    pair = jnp.concatenate(weights[:2], 1)
    for number, source in enumerate((tokens, core_tokens)):

        @pl.loop(0, 3)
        def _(step):
            start = pl.multiple_of(step * 256, 256)
            here = pl.ds(number * rows + start, 256)
            left = jnp.concatenate(
                [source[block, pl.ds(start, 256), :] for block in range(blocks)], 1
            )
            both = jnp.dot(left, pair, preferred_element_type=F32).astype(BF16)
            query[here, :] = both[:, :128]
            keys[here, :] = both[:, 128:]
            values[here, :] = jnp.dot(
                left, weights[2], preferred_element_type=F32
            ).astype(BF16)
            norms[here, :] = down_norm(both[:, 128:])


def summary_kernel(own, other, keys, values, norms, marks, pieces, flat, part):
    xl, c = lax.axis_index("xl"), lax.axis_index("c")
    flat[xl] = own[...].reshape(256, 128).astype(F32)
    flat[1 - xl] = other[...].reshape(256, 128).astype(F32)
    rows = []
    for side in range(2):
        for mark in range(4):
            first = flat[side, pl.ds(mark, 32, stride=8), :]
            second = flat[side, pl.ds(4 + mark, 32, stride=8), :]
            rows.append(jnp.where(c == 0, first, second))
    rows = jnp.concatenate(rows, 0).astype(BF16)
    marks[...] = rows
    weights = gauss(keys[...], rows, norms[...], side_norm(rows)).astype(BF16)
    part[...] = lax.dot_general(values[...], weights, COLS, preferred_element_type=F32)
    for half in range(2):
        for four in range(4):
            pieces[pl.ds(half * 4 + four, 32, stride=8), :] = part[
                pl.ds(four * 32, 32), pl.ds(half * 128, 128)
            ]


def parts(value):
    upper = value.astype(BF16)
    return upper, (value - upper.astype(F32)).astype(BF16)


def three(left, right):
    upper = jnp.dot(left[0], right[0], preferred_element_type=F32)
    cross = jnp.dot(left[0], right[1], preferred_element_type=F32)
    return upper + (cross + jnp.dot(left[1], right[0], preferred_element_type=F32))


def inverse_kernel(marks_ref, inverse_ref):
    marks = marks_ref[...]
    inner = gauss(marks, marks, down_norm(marks), side_norm(marks))
    scale_cols = jnp.max(jnp.sum(jnp.abs(inner), 0, keepdims=True), 1, keepdims=True)
    scale_rows = jnp.max(jnp.sum(jnp.abs(inner), 1, keepdims=True), 0, keepdims=True)
    iterate = inner / (scale_cols * scale_rows)
    inner = parts(inner)
    for step in range(NSTEPS):
        now = parts(iterate)
        iterate = 2.0 * iterate - three(parts(three(now, inner)), now)
    inverse_ref[...] = iterate


def mixed_kernel(pieces, inverse, spread):
    summed = jnp.sum(pieces[...], 0)
    left = high(summed, inverse[:, :128], ROWS)
    right = high(summed, inverse[:, 128:], ROWS)
    mixed = left[:4] + right[4:]
    chosen = jnp.concatenate([mixed[:, :128], mixed[:, 128:]], 0).astype(BF16)
    for place in range(spread.shape[0]):
        spread[place] = chosen


def query_weight_kernel(query, marks, weights):
    rows = marks[...]
    weights[...] = gauss(query[...], rows, down_norm(query[...]), side_norm(rows)).astype(BF16)


def give_kernel(spread, weights, mixed, give, flat):
    flat[...] = spread[...].reshape(256, 128).astype(F32)
    halves = [
        jnp.concatenate([flat[pl.ds(half * 4 + four, 32, stride=8), :] for four in range(4)], 0)
        for half in range(2)
    ]
    matrix = jnp.concatenate(halves, 1).astype(BF16)
    mixed[...] = matrix
    give[...] = lax.dot_general(
        weights[768:, :], matrix, ROWS, preferred_element_type=F32
    ).astype(BF16)


def keep_kernel(mixed, weights, keep):
    keep[...] = lax.dot_general(
        weights[:768, :], mixed[...], ROWS, preferred_element_type=F32
    ).astype(BF16)


def join_kernel(keep, received, out):
    c = lax.axis_index("c")
    out[:, pl.ds(pl.multiple_of(c * 128, 128), 128)] = keep[...]
    out[:, pl.ds(pl.multiple_of((1 - c) * 128, 128), 128)] = received[...]


def shape(dims, dtype):
    return jax.ShapeDtypeStruct(dims, dtype)


def shards(tokens, weights, landmark_pos):
    whole = lax.all_to_all(
        jnp.broadcast_to(tokens[None], (8,) + tokens.shape), HEAD, 0, 0, tiled=True
    )
    column = lax.all_gather(weights, "z", axis=1, tiled=True).reshape(3, 16, 32, 256)
    core = shift(column, "c", 1)
    core, later = lax.optimization_barrier((core, whole))
    core_tokens = shift(later, "c", 1)
    packed = call(
        pack_kernel,
        "pack",
        shape((2, 3, 16, 32, 128), BF16),
        [ANY, ANY],
        1 << 10,
        3 << 19,
        [pltpu.SemaphoreType.DMA((2,))],
        space=HBM,
    )(column, core)
    picked = call(
        pick_kernel,
        "pick",
        shape((8, 2048), BF16),
        [SMEM, ANY],
        1 << 20,
        1 << 19,
        [
            pltpu.VMEM((8, 8, 8, 256), BF16),
            pltpu.VMEM((8, 2048), F32),
            pltpu.SemaphoreType.DMA((8,)),
        ],
    )(landmark_pos, whole)
    other_picked = shift(picked, "xl", 1)
    keep, give = call(
        partial_kernel,
        "partial",
        (shape((8, 128), F32), shape((8, 128), F32)),
        [VMEM, VMEM, ANY, ANY],
        2 * 16 * 1024 * 512,
        1 << 20,
        [pltpu.VMEM((2, 16, 2, 32, 256), BF16), pltpu.SemaphoreType.DMA((2,))],
    )(picked, other_picked, column, core)
    received = shift(give, "xl", 1)
    spread = call(
        finish_kernel, "finish", shape((32, 8, 128), BF16), [VMEM] * 2, 1 << 14, 1 << 16
    )(keep, received)
    spread, packed = lax.optimization_barrier((spread, packed))
    own_marks = lax.all_to_all(spread, CORES, 0, 0, tiled=True)
    across = shift(packed, "xl", 1)
    query, keys, values, norms = call(
        project_kernel,
        "project",
        (
            shape((1536, 128), BF16),
            shape((1536, 128), BF16),
            shape((1536, 128), BF16),
            shape((1536, 1), F32),
        ),
        [VMEM, VMEM, ANY, ANY],
        2 * 1536 * 2048 * 384,
        8 << 20,
        [pltpu.VMEM((3, 16, 2, 2, 32, 128), BF16), pltpu.SemaphoreType.DMA((4,))],
    )(whole, core_tokens, packed, across)

    other_marks = shift(own_marks, "xl", 1)
    marks, chip = call(
        summary_kernel,
        "summary",
        (shape((256, 128), BF16), shape((256, 128), F32)),
        [VMEM] * 5,
        2 * 2 * 1536 * 256 * 128,
        2 << 20,
        [pltpu.VMEM((2, 256, 128), F32), pltpu.VMEM((128, 256), F32)],
        1536 * 256,
    )(own_marks, other_marks, keys, values, norms)
    chip, marks = lax.optimization_barrier((chip, marks))
    inverse = call(
        inverse_kernel,
        "inverse",
        shape((256, 256), F32),
        [VMEM],
        2 * 6 * 12 * 256**3,
        1 << 19,
        (),
        256 * 256,
    )(marks)
    pieces = lax.all_to_all(chip.reshape(32, 8, 128), CHIPS, 0, 0, tiled=True)
    spread = call(
        mixed_kernel,
        "mixed",
        shape((32, 8, 128), BF16),
        [VMEM] * 2,
        2 * 6 * 16 * 256 * 128,
        1 << 19,
    )(pieces, inverse)
    spread, marks = lax.optimization_barrier((spread, marks))
    spread = lax.all_to_all(spread, CHIPS, 0, 0, tiled=True)
    query_weights = call(
        query_weight_kernel,
        "query_weights",
        shape((1536, 256), BF16),
        [VMEM] * 2,
        2 * 1536 * 256 * 128,
        2 << 20,
        (),
        1536 * 256,
    )(query, marks)
    spread, query_weights = lax.optimization_barrier((spread, query_weights))
    mixed, give = call(
        give_kernel,
        "give",
        (shape((128, 256), BF16), shape((768, 128), BF16)),
        [VMEM] * 2,
        2 * 768 * 256 * 128,
        1 << 19,
        [pltpu.VMEM((256, 128), F32)],
    )(spread, query_weights)
    received = shift(give, "c", 1)
    keep = call(
        keep_kernel,
        "keep",
        shape((768, 128), BF16),
        [VMEM] * 2,
        2 * 768 * 256 * 128,
        1 << 19,
    )(mixed, query_weights)
    return call(
        join_kernel, "join", shape((768, 256), BF16), [VMEM] * 2, 1 << 10, 1 << 19
    )(keep, received)


def solution(mesh):
    fine = Mesh(mesh.devices.reshape(SIZES), AXES)
    return jax.shard_map(
        shards,
        mesh=fine,
        in_specs=(P(SEQ, HEAD), P(None, SEQ, HEAD), P(HEAD, None)),
        out_specs=P(SEQ, HEAD),
        check_vma=False,
    )
```

```python
import math

import jax
import jax.numpy as jnp
from jax import lax
from jax.experimental import pallas as pl
from jax.experimental.pallas import tpu as pltpu
from jax.sharding import Mesh
from jax.sharding import PartitionSpec as P

NSTEPS = 6
AXES = ("y", "xh", "z", "xl", "c")
SIZES = (4, 2, 16, 2, 2)
HEAD = ("y", "xh")
SEQ = ("z", "xl", "c")
CHIPS = ("z", "xl")

VMEM = pl.BlockSpec(memory_space=pltpu.VMEM)
SMEM = pl.BlockSpec(memory_space=pltpu.SMEM)
HBM = pl.BlockSpec(memory_space=pltpu.HBM)
ANY = pl.BlockSpec(memory_space=pl.ANY)
BF16 = jnp.bfloat16
F32 = jnp.float32
ROWS = (((1,), (1,)), ((), ()))
COLS = (((0,), (0,)), ((), ()))


def call(kernel, name, outs, ins, flops, nbytes, scratch=(), exps=0, space=VMEM):
    return pl.pallas_call(
        kernel,
        out_shape=outs,
        in_specs=ins,
        out_specs=jax.tree.map(lambda _: space, outs),
        scratch_shapes=list(scratch),
        cost_estimate=pl.CostEstimate(flops=flops, bytes_accessed=nbytes, transcendentals=exps),
        compiler_params=pltpu.CompilerParams(vmem_limit_bytes=16 << 20),
        name=name,
    )


def shift(value, axis, step):
    size = lax.axis_size(axis)
    return lax.ppermute(value, axis, [(i, (i + step) % size) for i in range(size)])


def high(left, right, dims=(((1,), (0,)), ((), ()))):
    return lax.dot_general(
        left, right, dims, precision=lax.Precision.HIGHEST, preferred_element_type=F32
    )


def side_norm(rows):
    rows32 = rows.astype(F32)
    ones = jnp.ones((8, rows.shape[1]), F32)
    return high(ones, rows32 * rows32, ROWS)[:1]


def down_norm(rows):
    rows32 = rows.astype(F32)
    return jnp.sum(rows32 * rows32, 1, keepdims=True)


def gauss(left, right, left_norm, right_norm):
    product = lax.dot_general(left, right, ROWS, preferred_element_type=F32)
    return jnp.exp((left_norm + right_norm - 2.0 * product) * (-0.5 / math.sqrt(left.shape[1])))


def run(copies):
    for copy in copies:
        copy.start()
    for copy in copies:
        copy.wait()


def pick_kernel(pos_ref, tokens, picked, groups, rows, sems):
    group = (lax.axis_index("z") * 2 + lax.axis_index("xl")) * 2 + lax.axis_index("c")
    blocks, count, width = tokens.shape
    places, copies = [], []
    for mark in range(8):
        row = pos_ref[mark // 4, group * 4 + mark % 4] - group * count
        start = pl.multiple_of((row // 8) * 8, 8)
        places.append(row - start)
        copies.append(
            pltpu.make_async_copy(
                tokens.at[:, pl.ds(start, 8), :], groups.at[mark], sems.at[mark]
            )
        )
    run(copies)
    index = lax.broadcasted_iota(jnp.int32, (8, width), 0)
    for mark, place in enumerate(places):
        for block in range(blocks):
            eight = groups[mark, block].astype(F32)
            rows[pl.ds(mark, 1), pl.ds(block * width, width)] = jnp.sum(
                jnp.where(index == place, eight, 0.0), 0, keepdims=True
            )
    picked[...] = rows[...].astype(BF16)


def partial_kernel(own, other, column, across, keep, give, w, sems):
    xl, c = lax.axis_index("xl"), lax.axis_index("c")
    run(
        [
            pltpu.make_async_copy(column.at[pl.ds(0, 2)], w.at[:, :, xl], sems.at[0]),
            pltpu.make_async_copy(across.at[pl.ds(0, 2)], w.at[:, :, 1 - xl], sems.at[1]),
        ]
    )
    rows = jnp.concatenate([own[...].astype(F32), other[...].astype(F32)], 0)
    quarter = lax.broadcasted_iota(jnp.int32, (16, 128), 1) // 32
    tiles = []
    for pair in range(8):
        even = rows[:, pair * 256 : pair * 256 + 128]
        odd = rows[:, pair * 256 + 128 : pair * 256 + 256]
        even1, odd1 = pltpu.roll(even, 96, 1), pltpu.roll(odd, 32, 1)
        first = (even, even1, pltpu.roll(odd, 64, 1), odd1)
        second = (even1, pltpu.roll(even, 64, 1), odd1, odd)
        zero, one = (
            jnp.where(
                quarter < 2,
                jnp.where(quarter == 0, four[0], four[1]),
                jnp.where(quarter == 2, four[2], four[3]),
            )
            for four in (first, second)
        )
        tiles.append(jnp.where(c == 0, zero, one))
    left = jnp.concatenate(tiles, 1).astype(BF16)
    results = [
        jnp.dot(left, w[kind].reshape(1024, 256), preferred_element_type=F32) for kind in range(2)
    ]
    number = lax.broadcasted_iota(jnp.int32, (16, 256), 0)
    both = jnp.where(number % 2 == 0, results[0], results[1])
    chosen = jnp.where((number[:, :128] % 8) < 4, both[:, :128], both[:, 128:])
    keep[...] = chosen[:8]
    give[...] = chosen[8:]


def finish_kernel(keep, received, spread):
    chosen = (keep[...] + received[...]).astype(BF16)
    for place in range(spread.shape[0]):
        spread[place] = chosen


def pack_kernel(column, across, packed, given, sems):
    xl, c = lax.axis_index("xl"), lax.axis_index("c")
    copies = []
    for target, head in ((packed, c), (given, 1 - c)):
        cols = pl.ds(pl.multiple_of(head * 128, 128), 128)
        for piece, side in ((column, xl), (across, 1 - xl)):
            copies.append(
                pltpu.make_async_copy(
                    piece.at[:, :, :, cols], target.at[side], sems.at[len(copies)]
                )
            )
    run(copies)


def project_kernel(tokens, core_tokens, packed, received, query, keys, values, norms, w, sems):
    c = lax.axis_index("c")
    copies = []
    for row in range(2):
        for source, part in ((packed, c), (received, 1 - c)):
            copies.append(
                pltpu.make_async_copy(
                    source.at[row], w.at[:, :, row, part], sems.at[len(copies)]
                )
            )
    run(copies)
    blocks, rows, width = tokens.shape
    weights = [w[kind].reshape(blocks * width, 128) for kind in range(3)]
    pair = jnp.concatenate(weights[:2], 1)
    for number, source in enumerate((tokens, core_tokens)):

        @pl.loop(0, 3)
        def _(step):
            start = pl.multiple_of(step * 256, 256)
            here = pl.ds(number * rows + start, 256)
            left = jnp.concatenate(
                [source[block, pl.ds(start, 256), :] for block in range(blocks)], 1
            )
            both = jnp.dot(left, pair, preferred_element_type=F32).astype(BF16)
            query[here, :] = both[:, :128]
            keys[here, :] = both[:, 128:]
            values[here, :] = jnp.dot(
                left, weights[2], preferred_element_type=F32
            ).astype(BF16)
            norms[here, :] = down_norm(both[:, 128:])


def summary_kernel(own, other, keys, values, norms, marks, pieces, flat, part):
    c = lax.axis_index("c")
    flat[c] = own[...].reshape(256, 128).astype(F32)
    flat[1 - c] = other[...].reshape(256, 128).astype(F32)
    rows = []
    for side in range(2):
        for mark in range(4):
            first = flat[side, pl.ds(mark, 32, stride=8), :]
            second = flat[side, pl.ds(4 + mark, 32, stride=8), :]
            rows.append(jnp.where(c == 0, first, second))
    rows = jnp.concatenate(rows, 0).astype(BF16)
    marks[...] = rows
    weights = gauss(keys[...], rows, norms[...], side_norm(rows)).astype(BF16)
    part[...] = lax.dot_general(values[...], weights, COLS, preferred_element_type=F32)
    for half in range(2):
        for four in range(4):
            pieces[pl.ds(half * 4 + four, 32, stride=8), :] = part[
                pl.ds(four * 32, 32), pl.ds(half * 128, 128)
            ]


def parts(value):
    upper = value.astype(BF16)
    return upper, (value - upper.astype(F32)).astype(BF16)


def three(left, right):
    upper = jnp.dot(left[0], right[0], preferred_element_type=F32)
    cross = jnp.dot(left[0], right[1], preferred_element_type=F32)
    return upper + (cross + jnp.dot(left[1], right[0], preferred_element_type=F32))


def inverse_kernel(marks_ref, inverse_ref):
    marks = marks_ref[...]
    inner = gauss(marks, marks, down_norm(marks), side_norm(marks))
    scale_cols = jnp.max(jnp.sum(jnp.abs(inner), 0, keepdims=True), 1, keepdims=True)
    scale_rows = jnp.max(jnp.sum(jnp.abs(inner), 1, keepdims=True), 0, keepdims=True)
    iterate = inner / (scale_cols * scale_rows)
    inner = parts(inner)
    for step in range(NSTEPS):
        now = parts(iterate)
        iterate = 2.0 * iterate - three(parts(three(now, inner)), now)
    inverse_ref[...] = iterate


def mixed_kernel(pieces, inverse, spread):
    summed = jnp.sum(pieces[...], 0)
    left = high(summed, inverse[:, :128], ROWS)
    right = high(summed, inverse[:, 128:], ROWS)
    mixed = left[:4] + right[4:]
    chosen = jnp.concatenate([mixed[:, :128], mixed[:, 128:]], 0).astype(BF16)
    for place in range(spread.shape[0]):
        spread[place] = chosen


def query_weight_kernel(query, marks, weights):
    rows = marks[...]
    weights[...] = gauss(query[...], rows, down_norm(query[...]), side_norm(rows)).astype(BF16)


def give_kernel(spread, weights, mixed, give, flat):
    flat[...] = spread[...].reshape(256, 128).astype(F32)
    halves = [
        jnp.concatenate([flat[pl.ds(half * 4 + four, 32, stride=8), :] for four in range(4)], 0)
        for half in range(2)
    ]
    matrix = jnp.concatenate(halves, 1).astype(BF16)
    mixed[...] = matrix
    give[...] = lax.dot_general(
        weights[768:, :], matrix, ROWS, preferred_element_type=F32
    ).astype(BF16)


def keep_kernel(mixed, weights, keep):
    keep[...] = lax.dot_general(
        weights[:768, :], mixed[...], ROWS, preferred_element_type=F32
    ).astype(BF16)


def join_kernel(keep, received, out):
    c = lax.axis_index("c")
    out[:, pl.ds(pl.multiple_of(c * 128, 128), 128)] = keep[...]
    out[:, pl.ds(pl.multiple_of((1 - c) * 128, 128), 128)] = received[...]


def shape(dims, dtype):
    return jax.ShapeDtypeStruct(dims, dtype)


def shards(tokens, weights, landmark_pos):
    whole = lax.all_to_all(
        jnp.broadcast_to(tokens[None], (8,) + tokens.shape), HEAD, 0, 0, tiled=True
    )
    column = lax.all_gather(weights, "z", axis=1, tiled=True).reshape(3, 16, 32, 256)
    landmark_pos, column = lax.optimization_barrier((landmark_pos, column))
    across = shift(column, "xl", 1)
    picked = call(
        pick_kernel,
        "pick",
        shape((8, 2048), BF16),
        [SMEM, ANY],
        1 << 20,
        1 << 19,
        [
            pltpu.VMEM((8, 8, 8, 256), BF16),
            pltpu.VMEM((8, 2048), F32),
            pltpu.SemaphoreType.DMA((8,)),
        ],
    )(landmark_pos, whole)
    other_picked = shift(picked, "c", 1)
    keep, give = call(
        partial_kernel,
        "partial",
        (shape((8, 128), F32), shape((8, 128), F32)),
        [VMEM, VMEM, ANY, ANY],
        2 * 16 * 1024 * 512,
        1 << 20,
        [pltpu.VMEM((2, 16, 2, 32, 256), BF16), pltpu.SemaphoreType.DMA((2,))],
    )(picked, other_picked, column, across)
    received = shift(give, "c", 1)
    column, across, whole, received = lax.optimization_barrier((column, across, whole, received))
    core_tokens = shift(whole, "c", 1)
    packed, given = call(
        pack_kernel,
        "pack",
        (shape((2, 3, 16, 32, 128), BF16), shape((2, 3, 16, 32, 128), BF16)),
        [ANY, ANY],
        1 << 10,
        3 << 19,
        [pltpu.SemaphoreType.DMA((4,))],
        space=HBM,
    )(column, across)
    core_weights = shift(given, "c", 1)
    spread = call(
        finish_kernel, "finish", shape((32, 8, 128), BF16), [VMEM] * 2, 1 << 14, 1 << 16
    )(keep, received)
    own_marks = lax.all_to_all(spread, CHIPS, 0, 0, tiled=True)
    query, keys, values, norms = call(
        project_kernel,
        "project",
        (
            shape((1536, 128), BF16),
            shape((1536, 128), BF16),
            shape((1536, 128), BF16),
            shape((1536, 1), F32),
        ),
        [VMEM, VMEM, ANY, ANY],
        2 * 1536 * 2048 * 384,
        8 << 20,
        [pltpu.VMEM((3, 16, 2, 2, 32, 128), BF16), pltpu.SemaphoreType.DMA((4,))],
    )(whole, core_tokens, packed, core_weights)

    other_marks = shift(own_marks, "c", 1)
    marks, chip = call(
        summary_kernel,
        "summary",
        (shape((256, 128), BF16), shape((256, 128), F32)),
        [VMEM] * 5,
        2 * 2 * 1536 * 256 * 128,
        2 << 20,
        [pltpu.VMEM((2, 256, 128), F32), pltpu.VMEM((128, 256), F32)],
        1536 * 256,
    )(own_marks, other_marks, keys, values, norms)
    chip, marks = lax.optimization_barrier((chip, marks))
    inverse = call(
        inverse_kernel,
        "inverse",
        shape((256, 256), F32),
        [VMEM],
        2 * 6 * 12 * 256**3,
        1 << 19,
        (),
        256 * 256,
    )(marks)
    pieces = lax.all_to_all(chip.reshape(32, 8, 128), CHIPS, 0, 0, tiled=True)
    spread = call(
        mixed_kernel,
        "mixed",
        shape((32, 8, 128), BF16),
        [VMEM] * 2,
        2 * 6 * 16 * 256 * 128,
        1 << 19,
    )(pieces, inverse)
    spread, marks = lax.optimization_barrier((spread, marks))
    spread = lax.all_to_all(spread, CHIPS, 0, 0, tiled=True)
    query_weights = call(
        query_weight_kernel,
        "query_weights",
        shape((1536, 256), BF16),
        [VMEM] * 2,
        2 * 1536 * 256 * 128,
        2 << 20,
        (),
        1536 * 256,
    )(query, marks)
    spread, query_weights = lax.optimization_barrier((spread, query_weights))
    mixed, give = call(
        give_kernel,
        "give",
        (shape((128, 256), BF16), shape((768, 128), BF16)),
        [VMEM] * 2,
        2 * 768 * 256 * 128,
        1 << 19,
        [pltpu.VMEM((256, 128), F32)],
    )(spread, query_weights)
    received = shift(give, "c", 1)
    keep = call(
        keep_kernel,
        "keep",
        shape((768, 128), BF16),
        [VMEM] * 2,
        2 * 768 * 256 * 128,
        1 << 19,
    )(mixed, query_weights)
    return call(
        join_kernel, "join", shape((768, 256), BF16), [VMEM] * 2, 1 << 10, 1 << 19
    )(keep, received)


def solution(mesh):
    fine = Mesh(mesh.devices.reshape(SIZES), AXES)
    return jax.shard_map(
        shards,
        mesh=fine,
        in_specs=(P(SEQ, HEAD), P(None, SEQ, HEAD), P(HEAD, None)),
        out_specs=P(SEQ, HEAD),
        check_vma=False,
    )
```

```python
import math

import jax
import jax.numpy as jnp
from jax import lax
from jax.experimental import pallas as pl
from jax.experimental.pallas import tpu as pltpu
from jax.sharding import Mesh
from jax.sharding import PartitionSpec as P

NSTEPS = 6
AXES = ("y", "xh", "z", "xl", "c")
SIZES = (4, 2, 16, 2, 2)
HEAD = ("y", "xh")
SEQ = ("z", "xl", "c")
CHIPS = ("z", "xl")
CORES = ("z", "c")

VMEM = pl.BlockSpec(memory_space=pltpu.VMEM)
SMEM = pl.BlockSpec(memory_space=pltpu.SMEM)
HBM = pl.BlockSpec(memory_space=pltpu.HBM)
ANY = pl.BlockSpec(memory_space=pl.ANY)
BF16 = jnp.bfloat16
F32 = jnp.float32
ROWS = (((1,), (1,)), ((), ()))
COLS = (((0,), (0,)), ((), ()))


def call(kernel, name, outs, ins, flops, nbytes, scratch=(), exps=0, space=VMEM):
    return pl.pallas_call(
        kernel,
        out_shape=outs,
        in_specs=ins,
        out_specs=jax.tree.map(lambda _: space, outs),
        scratch_shapes=list(scratch),
        cost_estimate=pl.CostEstimate(flops=flops, bytes_accessed=nbytes, transcendentals=exps),
        compiler_params=pltpu.CompilerParams(vmem_limit_bytes=16 << 20),
        name=name,
    )


def shift(value, axis, step):
    size = lax.axis_size(axis)
    return lax.ppermute(value, axis, [(i, (i + step) % size) for i in range(size)])


def high(left, right, dims=(((1,), (0,)), ((), ()))):
    return lax.dot_general(
        left, right, dims, precision=lax.Precision.HIGHEST, preferred_element_type=F32
    )


def side_norm(rows):
    rows32 = rows.astype(F32)
    ones = jnp.ones((8, rows.shape[1]), F32)
    return high(ones, rows32 * rows32, ROWS)[:1]


def down_norm(rows):
    rows32 = rows.astype(F32)
    return jnp.sum(rows32 * rows32, 1, keepdims=True)


def gauss(left, right, left_norm, right_norm):
    product = lax.dot_general(left, right, ROWS, preferred_element_type=F32)
    return jnp.exp((left_norm + right_norm - 2.0 * product) * (-0.5 / math.sqrt(left.shape[1])))


def run(copies):
    for copy in copies:
        copy.start()
    for copy in copies:
        copy.wait()


def pick_kernel(pos_ref, tokens, picked, groups, rows, sems):
    group = (lax.axis_index("z") * 2 + lax.axis_index("xl")) * 2 + lax.axis_index("c")
    blocks, count, width = tokens.shape
    places, copies = [], []
    for mark in range(8):
        row = pos_ref[mark // 4, group * 4 + mark % 4] - group * count
        start = pl.multiple_of((row // 8) * 8, 8)
        places.append(row - start)
        copies.append(
            pltpu.make_async_copy(
                tokens.at[:, pl.ds(start, 8), :], groups.at[mark], sems.at[mark]
            )
        )
    run(copies)
    index = lax.broadcasted_iota(jnp.int32, (8, width), 0)
    for mark, place in enumerate(places):
        for block in range(blocks):
            eight = groups[mark, block].astype(F32)
            rows[pl.ds(mark, 1), pl.ds(block * width, width)] = jnp.sum(
                jnp.where(index == place, eight, 0.0), 0, keepdims=True
            )
    picked[...] = rows[...].astype(BF16)


def partial_kernel(own, other, column, core, keep, give, packed, w, sems):
    xl, c = lax.axis_index("xl"), lax.axis_index("c")
    cols = pl.ds(pl.multiple_of(c * 128, 128), 128)
    packs = [
        pltpu.make_async_copy(column.at[:, :, :, cols], packed.at[c], sems.at[2]),
        pltpu.make_async_copy(core.at[:, :, :, cols], packed.at[1 - c], sems.at[3]),
    ]
    run(
        [
            pltpu.make_async_copy(column.at[pl.ds(0, 2)], w.at[:, :, c], sems.at[0]),
            pltpu.make_async_copy(core.at[pl.ds(0, 2)], w.at[:, :, 1 - c], sems.at[1]),
        ]
    )
    for copy in packs:
        copy.start()
    rows = jnp.concatenate([own[...].astype(F32), other[...].astype(F32)], 0)
    low = lax.broadcasted_iota(jnp.int32, (16, 128), 1) < 64
    tiles = []
    for pair in range(8):
        even = rows[:, pair * 256 : pair * 256 + 128]
        odd = rows[:, pair * 256 + 128 : pair * 256 + 256]
        first = jnp.where(low, even, pltpu.roll(odd, 64, 1))
        second = jnp.where(low, pltpu.roll(even, 64, 1), odd)
        tiles.append(jnp.where(xl == 0, first, second))
    left = jnp.concatenate(tiles, 1).astype(BF16)
    results = [
        jnp.dot(left, w[kind].reshape(1024, 256), preferred_element_type=F32) for kind in range(2)
    ]
    number = lax.broadcasted_iota(jnp.int32, (16, 256), 0)
    both = jnp.where(number % 2 == 0, results[0], results[1])
    chosen = jnp.where((number[:, :128] % 8) < 4, both[:, :128], both[:, 128:])
    keep[...] = chosen[:8]
    give[...] = chosen[8:]
    for copy in packs:
        copy.wait()


def finish_kernel(keep, received, spread):
    chosen = (keep[...] + received[...]).astype(BF16)
    for place in range(spread.shape[0]):
        spread[place] = chosen


def project_kernel(tokens, core_tokens, packed, across, query, keys, values, norms, w, sems):
    xl = lax.axis_index("xl")
    copies = []
    for part in range(2):
        for source, row in ((packed, xl), (across, 1 - xl)):
            copies.append(
                pltpu.make_async_copy(
                    source.at[part], w.at[:, :, row, part], sems.at[len(copies)]
                )
            )
    run(copies)
    blocks, rows, width = tokens.shape
    weights = [w[kind].reshape(blocks * width, 128) for kind in range(3)]
    pair = jnp.concatenate(weights[:2], 1)
    for number, source in enumerate((tokens, core_tokens)):

        @pl.loop(0, 3)
        def _(step):
            start = pl.multiple_of(step * 256, 256)
            here = pl.ds(number * rows + start, 256)
            left = jnp.concatenate(
                [source[block, pl.ds(start, 256), :] for block in range(blocks)], 1
            )
            both = jnp.dot(left, pair, preferred_element_type=F32).astype(BF16)
            query[here, :] = both[:, :128]
            keys[here, :] = both[:, 128:]
            values[here, :] = jnp.dot(
                left, weights[2], preferred_element_type=F32
            ).astype(BF16)
            norms[here, :] = down_norm(both[:, 128:])


def summary_kernel(own, other, keys, values, norms, marks, pieces, flat, part):
    xl, c = lax.axis_index("xl"), lax.axis_index("c")
    flat[xl] = own[...].reshape(256, 128).astype(F32)
    flat[1 - xl] = other[...].reshape(256, 128).astype(F32)
    rows = []
    for side in range(2):
        for mark in range(4):
            first = flat[side, pl.ds(mark, 32, stride=8), :]
            second = flat[side, pl.ds(4 + mark, 32, stride=8), :]
            rows.append(jnp.where(c == 0, first, second))
    rows = jnp.concatenate(rows, 0).astype(BF16)
    marks[...] = rows
    weights = gauss(keys[...], rows, norms[...], side_norm(rows)).astype(BF16)
    part[...] = lax.dot_general(values[...], weights, COLS, preferred_element_type=F32)
    for half in range(2):
        for four in range(4):
            pieces[pl.ds(half * 4 + four, 32, stride=8), :] = part[
                pl.ds(four * 32, 32), pl.ds(half * 128, 128)
            ]


def parts(value):
    upper = value.astype(BF16)
    return upper, (value - upper.astype(F32)).astype(BF16)


def three(left, right):
    upper = jnp.dot(left[0], right[0], preferred_element_type=F32)
    cross = jnp.dot(left[0], right[1], preferred_element_type=F32)
    return upper + (cross + jnp.dot(left[1], right[0], preferred_element_type=F32))


def inverse_kernel(marks_ref, inverse_ref):
    marks = marks_ref[...]
    inner = gauss(marks, marks, down_norm(marks), side_norm(marks))
    scale_cols = jnp.max(jnp.sum(jnp.abs(inner), 0, keepdims=True), 1, keepdims=True)
    scale_rows = jnp.max(jnp.sum(jnp.abs(inner), 1, keepdims=True), 0, keepdims=True)
    iterate = inner / (scale_cols * scale_rows)
    inner = parts(inner)
    for step in range(NSTEPS):
        now = parts(iterate)
        iterate = 2.0 * iterate - three(parts(three(now, inner)), now)
    inverse_ref[...] = iterate


def mixed_kernel(pieces, inverse, spread):
    summed = jnp.sum(pieces[...], 0)
    left = high(summed, inverse[:, :128], ROWS)
    right = high(summed, inverse[:, 128:], ROWS)
    mixed = left[:4] + right[4:]
    chosen = jnp.concatenate([mixed[:, :128], mixed[:, 128:]], 0).astype(BF16)
    for place in range(spread.shape[0]):
        spread[place] = chosen


def query_weight_kernel(query, marks, weights):
    rows = marks[...]
    weights[...] = gauss(query[...], rows, down_norm(query[...]), side_norm(rows)).astype(BF16)


def give_kernel(spread, weights, mixed, give, flat):
    flat[...] = spread[...].reshape(256, 128).astype(F32)
    halves = [
        jnp.concatenate([flat[pl.ds(half * 4 + four, 32, stride=8), :] for four in range(4)], 0)
        for half in range(2)
    ]
    matrix = jnp.concatenate(halves, 1).astype(BF16)
    mixed[...] = matrix
    give[...] = lax.dot_general(
        weights[768:, :], matrix, ROWS, preferred_element_type=F32
    ).astype(BF16)


def keep_kernel(mixed, weights, keep):
    keep[...] = lax.dot_general(
        weights[:768, :], mixed[...], ROWS, preferred_element_type=F32
    ).astype(BF16)


def join_kernel(keep, received, out):
    c = lax.axis_index("c")
    out[:, pl.ds(pl.multiple_of(c * 128, 128), 128)] = keep[...]
    out[:, pl.ds(pl.multiple_of((1 - c) * 128, 128), 128)] = received[...]


def shape(dims, dtype):
    return jax.ShapeDtypeStruct(dims, dtype)


def shards(tokens, weights, landmark_pos):
    whole = lax.all_to_all(
        jnp.broadcast_to(tokens[None], (8,) + tokens.shape), HEAD, 0, 0, tiled=True
    )
    column = lax.all_gather(weights, "z", axis=1, tiled=True).reshape(3, 16, 32, 256)
    core = shift(column, "c", 1)
    core, later = lax.optimization_barrier((core, whole))
    core_tokens = shift(later, "c", 1)
    picked = call(
        pick_kernel,
        "pick",
        shape((8, 2048), BF16),
        [SMEM, ANY],
        1 << 20,
        1 << 19,
        [
            pltpu.VMEM((8, 8, 8, 256), BF16),
            pltpu.VMEM((8, 2048), F32),
            pltpu.SemaphoreType.DMA((8,)),
        ],
    )(landmark_pos, whole)
    other_picked = shift(picked, "xl", 1)
    keep, give, packed = call(
        partial_kernel,
        "partial",
        (shape((8, 128), F32), shape((8, 128), F32), shape((2, 3, 16, 32, 128), BF16)),
        [VMEM, VMEM, ANY, ANY],
        1 << 36,
        1 << 20,
        [pltpu.VMEM((2, 16, 2, 32, 256), BF16), pltpu.SemaphoreType.DMA((4,))],
    )(picked, other_picked, column, core)
    received = shift(give, "xl", 1)
    across = shift(packed, "xl", 1)
    spread = call(
        finish_kernel, "finish", shape((32, 8, 128), BF16), [VMEM] * 2, 1 << 34, 1 << 16
    )(keep, received)
    own_marks = lax.all_to_all(spread, CORES, 0, 0, tiled=True)
    query, keys, values, norms = call(
        project_kernel,
        "project",
        (
            shape((1536, 128), BF16),
            shape((1536, 128), BF16),
            shape((1536, 128), BF16),
            shape((1536, 1), F32),
        ),
        [VMEM, VMEM, ANY, ANY],
        2 * 1536 * 2048 * 384,
        8 << 20,
        [pltpu.VMEM((3, 16, 2, 2, 32, 128), BF16), pltpu.SemaphoreType.DMA((4,))],
    )(whole, core_tokens, packed, across)

    other_marks = shift(own_marks, "xl", 1)
    marks, chip = call(
        summary_kernel,
        "summary",
        (shape((256, 128), BF16), shape((256, 128), F32)),
        [VMEM] * 5,
        2 * 2 * 1536 * 256 * 128,
        2 << 20,
        [pltpu.VMEM((2, 256, 128), F32), pltpu.VMEM((128, 256), F32)],
        1536 * 256,
    )(own_marks, other_marks, keys, values, norms)
    chip, marks = lax.optimization_barrier((chip, marks))
    inverse = call(
        inverse_kernel,
        "inverse",
        shape((256, 256), F32),
        [VMEM],
        2 * 6 * 12 * 256**3,
        1 << 19,
        (),
        256 * 256,
    )(marks)
    pieces = lax.all_to_all(chip.reshape(32, 8, 128), CHIPS, 0, 0, tiled=True)
    spread = call(
        mixed_kernel,
        "mixed",
        shape((32, 8, 128), BF16),
        [VMEM] * 2,
        2 * 6 * 16 * 256 * 128,
        1 << 19,
    )(pieces, inverse)
    spread, marks = lax.optimization_barrier((spread, marks))
    spread = lax.all_to_all(spread, CHIPS, 0, 0, tiled=True)
    query_weights = call(
        query_weight_kernel,
        "query_weights",
        shape((1536, 256), BF16),
        [VMEM] * 2,
        2 * 1536 * 256 * 128,
        2 << 20,
        (),
        1536 * 256,
    )(query, marks)
    spread, query_weights = lax.optimization_barrier((spread, query_weights))
    mixed, give = call(
        give_kernel,
        "give",
        (shape((128, 256), BF16), shape((768, 128), BF16)),
        [VMEM] * 2,
        2 * 768 * 256 * 128,
        1 << 19,
        [pltpu.VMEM((256, 128), F32)],
    )(spread, query_weights)
    received = shift(give, "c", 1)
    keep = call(
        keep_kernel,
        "keep",
        shape((768, 128), BF16),
        [VMEM] * 2,
        2 * 768 * 256 * 128,
        1 << 19,
    )(mixed, query_weights)
    return call(
        join_kernel, "join", shape((768, 256), BF16), [VMEM] * 2, 1 << 10, 1 << 19
    )(keep, received)


def solution(mesh):
    fine = Mesh(mesh.devices.reshape(SIZES), AXES)
    return jax.shard_map(
        shards,
        mesh=fine,
        in_specs=(P(SEQ, HEAD), P(None, SEQ, HEAD), P(HEAD, None)),
        out_specs=P(SEQ, HEAD),
        check_vma=False,
    )
```

```python
import math

import jax
import jax.numpy as jnp
from jax import lax
from jax.experimental import pallas as pl
from jax.experimental.pallas import tpu as pltpu
from jax.sharding import Mesh
from jax.sharding import PartitionSpec as P

NSTEPS = 6
AXES = ("y", "xh", "z", "xl", "c")
SIZES = (4, 2, 16, 2, 2)
HEAD = ("y", "xh")
SEQ = ("z", "xl", "c")
CHIPS = ("z", "xl")
CORES = ("z", "c")

VMEM = pl.BlockSpec(memory_space=pltpu.VMEM)
SMEM = pl.BlockSpec(memory_space=pltpu.SMEM)
HBM = pl.BlockSpec(memory_space=pltpu.HBM)
ANY = pl.BlockSpec(memory_space=pl.ANY)
BF16 = jnp.bfloat16
F32 = jnp.float32
ROWS = (((1,), (1,)), ((), ()))
COLS = (((0,), (0,)), ((), ()))


def call(kernel, name, outs, ins, flops, nbytes, scratch=(), exps=0, space=VMEM):
    return pl.pallas_call(
        kernel,
        out_shape=outs,
        in_specs=ins,
        out_specs=jax.tree.map(lambda _: space, outs),
        scratch_shapes=list(scratch),
        cost_estimate=pl.CostEstimate(flops=flops, bytes_accessed=nbytes, transcendentals=exps),
        compiler_params=pltpu.CompilerParams(vmem_limit_bytes=16 << 20),
        name=name,
    )


def shift(value, axis, step):
    size = lax.axis_size(axis)
    return lax.ppermute(value, axis, [(i, (i + step) % size) for i in range(size)])


def high(left, right, dims=(((1,), (0,)), ((), ()))):
    return lax.dot_general(
        left, right, dims, precision=lax.Precision.HIGHEST, preferred_element_type=F32
    )


def side_norm(rows):
    rows32 = rows.astype(F32)
    ones = jnp.ones((8, rows.shape[1]), F32)
    return high(ones, rows32 * rows32, ROWS)[:1]


def down_norm(rows):
    rows32 = rows.astype(F32)
    return jnp.sum(rows32 * rows32, 1, keepdims=True)


def gauss(left, right, left_norm, right_norm):
    product = lax.dot_general(left, right, ROWS, preferred_element_type=F32)
    return jnp.exp((left_norm + right_norm - 2.0 * product) * (-0.5 / math.sqrt(left.shape[1])))


def run(copies):
    for copy in copies:
        copy.start()
    for copy in copies:
        copy.wait()


def stage_kernel(source, target, sems):
    run([pltpu.make_async_copy(source.at[i], target.at[i], sems.at[i]) for i in range(3)])


def pick_kernel(pos_ref, tokens, picked, groups, rows, sems):
    group = (lax.axis_index("z") * 2 + lax.axis_index("xl")) * 2 + lax.axis_index("c")
    blocks, count, width = tokens.shape
    places, copies = [], []
    for mark in range(8):
        row = pos_ref[mark // 4, group * 4 + mark % 4] - group * count
        start = pl.multiple_of((row // 8) * 8, 8)
        places.append(row - start)
        copies.append(
            pltpu.make_async_copy(
                tokens.at[:, pl.ds(start, 8), :], groups.at[mark], sems.at[mark]
            )
        )
    run(copies)
    index = lax.broadcasted_iota(jnp.int32, (8, width), 0)
    for mark, place in enumerate(places):
        for block in range(blocks):
            eight = groups[mark, block].astype(F32)
            rows[pl.ds(mark, 1), pl.ds(block * width, width)] = jnp.sum(
                jnp.where(index == place, eight, 0.0), 0, keepdims=True
            )
    picked[...] = rows[...].astype(BF16)


def prepare_kernel(column, core, w, packed, sems):
    c = lax.axis_index("c")
    cols = pl.ds(pl.multiple_of(c * 128, 128), 128)
    run(
        [
            pltpu.make_async_copy(column.at[pl.ds(0, 2)], w.at[:, :, c], sems.at[0]),
            pltpu.make_async_copy(core.at[pl.ds(0, 2)], w.at[:, :, 1 - c], sems.at[1]),
            pltpu.make_async_copy(column.at[:, :, :, cols], packed.at[c], sems.at[2]),
            pltpu.make_async_copy(core.at[:, :, :, cols], packed.at[1 - c], sems.at[3]),
        ]
    )


def partial_kernel(own, other, w, keep, give):
    xl = lax.axis_index("xl")
    rows = jnp.concatenate([own[...].astype(F32), other[...].astype(F32)], 0)
    low = lax.broadcasted_iota(jnp.int32, (16, 128), 1) < 64
    tiles = []
    for pair in range(8):
        even = rows[:, pair * 256 : pair * 256 + 128]
        odd = rows[:, pair * 256 + 128 : pair * 256 + 256]
        first = jnp.where(low, even, pltpu.roll(odd, 64, 1))
        second = jnp.where(low, pltpu.roll(even, 64, 1), odd)
        tiles.append(jnp.where(xl == 0, first, second))
    left = jnp.concatenate(tiles, 1).astype(BF16)
    results = [
        jnp.dot(left, w[kind].reshape(1024, 256), preferred_element_type=F32) for kind in range(2)
    ]
    number = lax.broadcasted_iota(jnp.int32, (16, 256), 0)
    both = jnp.where(number % 2 == 0, results[0], results[1])
    chosen = jnp.where((number[:, :128] % 8) < 4, both[:, :128], both[:, 128:])
    keep[...] = chosen[:8]
    give[...] = chosen[8:]


def finish_kernel(keep, received, spread):
    chosen = (keep[...] + received[...]).astype(BF16)
    for place in range(spread.shape[0]):
        spread[place] = chosen


def project_kernel(tokens, core_tokens, packed, across, query, keys, values, norms, w, sems):
    xl = lax.axis_index("xl")
    copies = []
    for part in range(2):
        for source, row in ((packed, xl), (across, 1 - xl)):
            copies.append(
                pltpu.make_async_copy(
                    source.at[part], w.at[:, :, row, part], sems.at[len(copies)]
                )
            )
    run(copies)
    blocks, rows, width = tokens.shape
    weights = [w[kind].reshape(blocks * width, 128) for kind in range(3)]
    pair = jnp.concatenate(weights[:2], 1)
    for number, source in enumerate((tokens, core_tokens)):

        @pl.loop(0, 3)
        def _(step):
            start = pl.multiple_of(step * 256, 256)
            here = pl.ds(number * rows + start, 256)
            left = jnp.concatenate(
                [source[block, pl.ds(start, 256), :] for block in range(blocks)], 1
            )
            both = jnp.dot(left, pair, preferred_element_type=F32).astype(BF16)
            query[here, :] = both[:, :128]
            keys[here, :] = both[:, 128:]
            values[here, :] = jnp.dot(
                left, weights[2], preferred_element_type=F32
            ).astype(BF16)
            norms[here, :] = down_norm(both[:, 128:])


def summary_kernel(own, other, keys, values, norms, marks, pieces, flat, part):
    xl, c = lax.axis_index("xl"), lax.axis_index("c")
    flat[xl] = own[...].reshape(256, 128).astype(F32)
    flat[1 - xl] = other[...].reshape(256, 128).astype(F32)
    rows = []
    for side in range(2):
        for mark in range(4):
            first = flat[side, pl.ds(mark, 32, stride=8), :]
            second = flat[side, pl.ds(4 + mark, 32, stride=8), :]
            rows.append(jnp.where(c == 0, first, second))
    rows = jnp.concatenate(rows, 0).astype(BF16)
    marks[...] = rows
    weights = gauss(keys[...], rows, norms[...], side_norm(rows)).astype(BF16)
    part[...] = lax.dot_general(values[...], weights, COLS, preferred_element_type=F32)
    for half in range(2):
        for four in range(4):
            pieces[pl.ds(half * 4 + four, 32, stride=8), :] = part[
                pl.ds(four * 32, 32), pl.ds(half * 128, 128)
            ]


def parts(value):
    upper = value.astype(BF16)
    return upper, (value - upper.astype(F32)).astype(BF16)


def three(left, right):
    upper = jnp.dot(left[0], right[0], preferred_element_type=F32)
    cross = jnp.dot(left[0], right[1], preferred_element_type=F32)
    return upper + (cross + jnp.dot(left[1], right[0], preferred_element_type=F32))


def inverse_kernel(marks_ref, inverse_ref):
    marks = marks_ref[...]
    inner = gauss(marks, marks, down_norm(marks), side_norm(marks))
    scale_cols = jnp.max(jnp.sum(jnp.abs(inner), 0, keepdims=True), 1, keepdims=True)
    scale_rows = jnp.max(jnp.sum(jnp.abs(inner), 1, keepdims=True), 0, keepdims=True)
    iterate = inner / (scale_cols * scale_rows)
    inner = parts(inner)
    for step in range(NSTEPS):
        now = parts(iterate)
        iterate = 2.0 * iterate - three(parts(three(now, inner)), now)
    inverse_ref[...] = iterate


def mixed_kernel(pieces, inverse, spread):
    summed = jnp.sum(pieces[...], 0)
    left = high(summed, inverse[:, :128], ROWS)
    right = high(summed, inverse[:, 128:], ROWS)
    mixed = left[:4] + right[4:]
    chosen = jnp.concatenate([mixed[:, :128], mixed[:, 128:]], 0).astype(BF16)
    for place in range(spread.shape[0]):
        spread[place] = chosen


def query_weight_kernel(query, marks, weights):
    rows = marks[...]
    weights[...] = gauss(query[...], rows, down_norm(query[...]), side_norm(rows)).astype(BF16)


def give_kernel(spread, weights, mixed, give, flat):
    flat[...] = spread[...].reshape(256, 128).astype(F32)
    halves = [
        jnp.concatenate([flat[pl.ds(half * 4 + four, 32, stride=8), :] for four in range(4)], 0)
        for half in range(2)
    ]
    matrix = jnp.concatenate(halves, 1).astype(BF16)
    mixed[...] = matrix
    give[...] = lax.dot_general(
        weights[768:, :], matrix, ROWS, preferred_element_type=F32
    ).astype(BF16)


def keep_kernel(mixed, weights, keep):
    keep[...] = lax.dot_general(
        weights[:768, :], mixed[...], ROWS, preferred_element_type=F32
    ).astype(BF16)


def join_kernel(keep, received, out):
    c = lax.axis_index("c")
    out[:, pl.ds(pl.multiple_of(c * 128, 128), 128)] = keep[...]
    out[:, pl.ds(pl.multiple_of((1 - c) * 128, 128), 128)] = received[...]


def shape(dims, dtype):
    return jax.ShapeDtypeStruct(dims, dtype)


def in_hbm(*values):
    return tuple(pltpu.with_memory_space_constraint(value, pltpu.HBM) for value in values)


def shards(tokens, weights, landmark_pos):
    whole = lax.all_to_all(
        jnp.broadcast_to(tokens[None], (8,) + tokens.shape), HEAD, 0, 0, tiled=True
    )
    column = lax.all_gather(weights, "z", axis=1, tiled=True).reshape(3, 16, 32, 256)
    column = call(
        stage_kernel,
        "stage",
        shape((3, 16, 32, 256), BF16),
        [VMEM],
        1 << 10,
        3 << 19,
        [pltpu.SemaphoreType.DMA((3,))],
        space=HBM,
    )(column)
    core = shift(column, "c", 1)
    column, core = in_hbm(column, core)
    core, later = lax.optimization_barrier((core, whole))
    core_tokens = shift(later, "c", 1)
    wide, packed = call(
        prepare_kernel,
        "prepare",
        (shape((2, 16, 2, 32, 256), BF16), shape((2, 3, 16, 32, 128), BF16)),
        [ANY, ANY],
        1 << 10,
        3 << 20,
        [pltpu.SemaphoreType.DMA((4,))],
    )(column, core)
    landmark_pos, wide = lax.optimization_barrier((landmark_pos, wide))
    picked = call(
        pick_kernel,
        "pick",
        shape((8, 2048), BF16),
        [SMEM, ANY],
        1 << 20,
        1 << 19,
        [
            pltpu.VMEM((8, 8, 8, 256), BF16),
            pltpu.VMEM((8, 2048), F32),
            pltpu.SemaphoreType.DMA((8,)),
        ],
    )(landmark_pos, whole)
    other_picked = shift(picked, "xl", 1)
    keep, give = call(
        partial_kernel,
        "partial",
        (shape((8, 128), F32), shape((8, 128), F32)),
        [VMEM, VMEM, VMEM],
        1 << 36,
        1 << 20,
    )(picked, other_picked, wide)
    packed, give = lax.optimization_barrier((packed, give))
    received = shift(give, "xl", 1)
    across = shift(packed, "xl", 1)
    spread = call(
        finish_kernel, "finish", shape((32, 8, 128), BF16), [VMEM] * 2, 1 << 34, 1 << 16
    )(keep, received)
    own_marks = lax.all_to_all(spread, CORES, 0, 0, tiled=True)
    query, keys, values, norms = call(
        project_kernel,
        "project",
        (
            shape((1536, 128), BF16),
            shape((1536, 128), BF16),
            shape((1536, 128), BF16),
            shape((1536, 1), F32),
        ),
        [VMEM, VMEM, ANY, ANY],
        2 * 1536 * 2048 * 384,
        8 << 20,
        [pltpu.VMEM((3, 16, 2, 2, 32, 128), BF16), pltpu.SemaphoreType.DMA((4,))],
    )(whole, core_tokens, packed, across)

    other_marks = shift(own_marks, "xl", 1)
    marks, chip = call(
        summary_kernel,
        "summary",
        (shape((256, 128), BF16), shape((256, 128), F32)),
        [VMEM] * 5,
        2 * 2 * 1536 * 256 * 128,
        2 << 20,
        [pltpu.VMEM((2, 256, 128), F32), pltpu.VMEM((128, 256), F32)],
        1536 * 256,
    )(own_marks, other_marks, keys, values, norms)
    chip, marks = lax.optimization_barrier((chip, marks))
    inverse = call(
        inverse_kernel,
        "inverse",
        shape((256, 256), F32),
        [VMEM],
        2 * 6 * 12 * 256**3,
        1 << 19,
        (),
        256 * 256,
    )(marks)
    pieces = lax.all_to_all(chip.reshape(32, 8, 128), CHIPS, 0, 0, tiled=True)
    spread = call(
        mixed_kernel,
        "mixed",
        shape((32, 8, 128), BF16),
        [VMEM] * 2,
        2 * 6 * 16 * 256 * 128,
        1 << 19,
    )(pieces, inverse)
    spread, marks = lax.optimization_barrier((spread, marks))
    spread = lax.all_to_all(spread, CHIPS, 0, 0, tiled=True)
    query_weights = call(
        query_weight_kernel,
        "query_weights",
        shape((1536, 256), BF16),
        [VMEM] * 2,
        2 * 1536 * 256 * 128,
        2 << 20,
        (),
        1536 * 256,
    )(query, marks)
    spread, query_weights = lax.optimization_barrier((spread, query_weights))
    mixed, give = call(
        give_kernel,
        "give",
        (shape((128, 256), BF16), shape((768, 128), BF16)),
        [VMEM] * 2,
        2 * 768 * 256 * 128,
        1 << 19,
        [pltpu.VMEM((256, 128), F32)],
    )(spread, query_weights)
    received = shift(give, "c", 1)
    keep = call(
        keep_kernel,
        "keep",
        shape((768, 128), BF16),
        [VMEM] * 2,
        2 * 768 * 256 * 128,
        1 << 19,
    )(mixed, query_weights)
    return call(
        join_kernel, "join", shape((768, 256), BF16), [VMEM] * 2, 1 << 10, 1 << 19
    )(keep, received)


def solution(mesh):
    fine = Mesh(mesh.devices.reshape(SIZES), AXES)
    return jax.shard_map(
        shards,
        mesh=fine,
        in_specs=(P(SEQ, HEAD), P(None, SEQ, HEAD), P(HEAD, None)),
        out_specs=P(SEQ, HEAD),
        check_vma=False,
    )
```

```python
import math

import jax
import jax.numpy as jnp
from jax import lax
from jax.experimental import pallas as pl
from jax.experimental.pallas import tpu as pltpu
from jax.sharding import Mesh
from jax.sharding import PartitionSpec as P

NSTEPS = 6
AXES = ("y", "xh", "z", "xl", "c")
SIZES = (4, 2, 16, 2, 2)
HEAD = ("y", "xh")
SEQ = ("z", "xl", "c")
CHIPS = ("z", "xl")
CORES = ("z", "c")

VMEM = pl.BlockSpec(memory_space=pltpu.VMEM)
SMEM = pl.BlockSpec(memory_space=pltpu.SMEM)
HBM = pl.BlockSpec(memory_space=pltpu.HBM)
ANY = pl.BlockSpec(memory_space=pl.ANY)
BF16 = jnp.bfloat16
F32 = jnp.float32
ROWS = (((1,), (1,)), ((), ()))
COLS = (((0,), (0,)), ((), ()))


def call(kernel, name, outs, ins, flops, nbytes, scratch=(), exps=0, space=VMEM):
    return pl.pallas_call(
        kernel,
        out_shape=outs,
        in_specs=ins,
        out_specs=jax.tree.map(lambda _: space, outs),
        scratch_shapes=list(scratch),
        cost_estimate=pl.CostEstimate(flops=flops, bytes_accessed=nbytes, transcendentals=exps),
        compiler_params=pltpu.CompilerParams(vmem_limit_bytes=16 << 20),
        name=name,
    )


def shift(value, axis, step):
    size = lax.axis_size(axis)
    return lax.ppermute(value, axis, [(i, (i + step) % size) for i in range(size)])


def high(left, right, dims=(((1,), (0,)), ((), ()))):
    return lax.dot_general(
        left, right, dims, precision=lax.Precision.HIGHEST, preferred_element_type=F32
    )


def side_norm(rows):
    rows32 = rows.astype(F32)
    ones = jnp.ones((8, rows.shape[1]), F32)
    return high(ones, rows32 * rows32, ROWS)[:1]


def down_norm(rows):
    rows32 = rows.astype(F32)
    return jnp.sum(rows32 * rows32, 1, keepdims=True)


def gauss(left, right, left_norm, right_norm):
    product = lax.dot_general(left, right, ROWS, preferred_element_type=F32)
    return jnp.exp((left_norm + right_norm - 2.0 * product) * (-0.5 / math.sqrt(left.shape[1])))


def run(copies):
    for copy in copies:
        copy.start()
    for copy in copies:
        copy.wait()


def stage_kernel(source, target, sems):
    run([pltpu.make_async_copy(source.at[i], target.at[i], sems.at[i]) for i in range(3)])


def pick_kernel(pos_ref, tokens, picked, groups, rows, sems):
    group = (lax.axis_index("z") * 2 + lax.axis_index("xl")) * 2 + lax.axis_index("c")
    blocks, count, width = tokens.shape
    places, copies = [], []
    for mark in range(8):
        row = pos_ref[mark // 4, group * 4 + mark % 4] - group * count
        start = pl.multiple_of((row // 8) * 8, 8)
        places.append(row - start)
        copies.append(
            pltpu.make_async_copy(
                tokens.at[:, pl.ds(start, 8), :], groups.at[mark], sems.at[mark]
            )
        )
    run(copies)
    index = lax.broadcasted_iota(jnp.int32, (8, width), 0)
    for mark, place in enumerate(places):
        for block in range(blocks):
            eight = groups[mark, block].astype(F32)
            rows[pl.ds(mark, 1), pl.ds(block * width, width)] = jnp.sum(
                jnp.where(index == place, eight, 0.0), 0, keepdims=True
            )
    picked[...] = rows[...].astype(BF16)


def prepare_kernel(column, core, w, packed, sems):
    c = lax.axis_index("c")
    cols = pl.ds(pl.multiple_of(c * 128, 128), 128)
    run(
        [
            pltpu.make_async_copy(column.at[pl.ds(0, 2)], w.at[:, :, c], sems.at[0]),
            pltpu.make_async_copy(core.at[pl.ds(0, 2)], w.at[:, :, 1 - c], sems.at[1]),
            pltpu.make_async_copy(column.at[:, :, :, cols], packed.at[c], sems.at[2]),
            pltpu.make_async_copy(core.at[:, :, :, cols], packed.at[1 - c], sems.at[3]),
        ]
    )


def partial_kernel(own, other, w, keep, give):
    xl = lax.axis_index("xl")
    rows = jnp.concatenate([own[...].astype(F32), other[...].astype(F32)], 0)
    low = lax.broadcasted_iota(jnp.int32, (16, 128), 1) < 64
    tiles = []
    for pair in range(8):
        even = rows[:, pair * 256 : pair * 256 + 128]
        odd = rows[:, pair * 256 + 128 : pair * 256 + 256]
        first = jnp.where(low, even, pltpu.roll(odd, 64, 1))
        second = jnp.where(low, pltpu.roll(even, 64, 1), odd)
        tiles.append(jnp.where(xl == 0, first, second))
    left = jnp.concatenate(tiles, 1).astype(BF16)
    results = [
        jnp.dot(left, w[kind].reshape(1024, 256), preferred_element_type=F32) for kind in range(2)
    ]
    number = lax.broadcasted_iota(jnp.int32, (16, 256), 0)
    both = jnp.where(number % 2 == 0, results[0], results[1])
    chosen = jnp.where((number[:, :128] % 8) < 4, both[:, :128], both[:, 128:])
    keep[...] = chosen[:8]
    give[...] = chosen[8:]


def finish_kernel(keep, received, spread):
    chosen = (keep[...] + received[...]).astype(BF16)
    for place in range(spread.shape[0]):
        spread[place] = chosen


def project_kernel(tokens, core_tokens, packed, across, query, keys, values, norms, w, sems):
    xl = lax.axis_index("xl")
    copies = []
    for part in range(2):
        for source, row in ((packed, xl), (across, 1 - xl)):
            copies.append(
                pltpu.make_async_copy(
                    source.at[part], w.at[:, :, row, part], sems.at[len(copies)]
                )
            )
    run(copies)
    blocks, rows, width = tokens.shape
    weights = [w[kind].reshape(blocks * width, 128) for kind in range(3)]
    pair = jnp.concatenate(weights[:2], 1)
    for number, source in enumerate((tokens, core_tokens)):

        @pl.loop(0, 3)
        def _(step):
            start = pl.multiple_of(step * 256, 256)
            here = pl.ds(number * rows + start, 256)
            left = jnp.concatenate(
                [source[block, pl.ds(start, 256), :] for block in range(blocks)], 1
            )
            both = jnp.dot(left, pair, preferred_element_type=F32).astype(BF16)
            query[here, :] = both[:, :128]
            keys[here, :] = both[:, 128:]
            values[here, :] = jnp.dot(
                left, weights[2], preferred_element_type=F32
            ).astype(BF16)
            norms[here, :] = down_norm(both[:, 128:])


def summary_kernel(own, other, keys, values, norms, marks, pieces, flat, part):
    xl, c = lax.axis_index("xl"), lax.axis_index("c")
    flat[xl] = own[...].reshape(256, 128).astype(F32)
    flat[1 - xl] = other[...].reshape(256, 128).astype(F32)
    rows = []
    for side in range(2):
        for mark in range(4):
            first = flat[side, pl.ds(mark, 32, stride=8), :]
            second = flat[side, pl.ds(4 + mark, 32, stride=8), :]
            rows.append(jnp.where(c == 0, first, second))
    rows = jnp.concatenate(rows, 0).astype(BF16)
    marks[...] = rows
    weights = gauss(keys[...], rows, norms[...], side_norm(rows)).astype(BF16)
    part[...] = lax.dot_general(values[...], weights, COLS, preferred_element_type=F32)
    for half in range(2):
        for four in range(4):
            pieces[pl.ds(half * 4 + four, 32, stride=8), :] = part[
                pl.ds(four * 32, 32), pl.ds(half * 128, 128)
            ]


def parts(value):
    upper = value.astype(BF16)
    return upper, (value - upper.astype(F32)).astype(BF16)


def three(left, right):
    upper = jnp.dot(left[0], right[0], preferred_element_type=F32)
    cross = jnp.dot(left[0], right[1], preferred_element_type=F32)
    return upper + (cross + jnp.dot(left[1], right[0], preferred_element_type=F32))


def inverse_kernel(marks_ref, inverse_ref):
    marks = marks_ref[...]
    inner = gauss(marks, marks, down_norm(marks), side_norm(marks))
    scale_cols = jnp.max(jnp.sum(jnp.abs(inner), 0, keepdims=True), 1, keepdims=True)
    scale_rows = jnp.max(jnp.sum(jnp.abs(inner), 1, keepdims=True), 0, keepdims=True)
    iterate = inner / (scale_cols * scale_rows)
    inner = parts(inner)
    for step in range(NSTEPS):
        now = parts(iterate)
        iterate = 2.0 * iterate - three(parts(three(now, inner)), now)
    inverse_ref[...] = iterate


def mixed_kernel(pieces, inverse, spread):
    summed = jnp.sum(pieces[...], 0)
    left = high(summed, inverse[:, :128], ROWS)
    right = high(summed, inverse[:, 128:], ROWS)
    mixed = left[:4] + right[4:]
    chosen = jnp.concatenate([mixed[:, :128], mixed[:, 128:]], 0).astype(BF16)
    for place in range(spread.shape[0]):
        spread[place] = chosen


def query_weight_kernel(query, marks, weights):
    rows = marks[...]
    weights[...] = gauss(query[...], rows, down_norm(query[...]), side_norm(rows)).astype(BF16)


def give_kernel(spread, weights, mixed, give, flat):
    flat[...] = spread[...].reshape(256, 128).astype(F32)
    halves = [
        jnp.concatenate([flat[pl.ds(half * 4 + four, 32, stride=8), :] for four in range(4)], 0)
        for half in range(2)
    ]
    matrix = jnp.concatenate(halves, 1).astype(BF16)
    mixed[...] = matrix
    give[...] = lax.dot_general(
        weights[768:, :], matrix, ROWS, preferred_element_type=F32
    ).astype(BF16)


def keep_kernel(mixed, weights, keep):
    keep[...] = lax.dot_general(
        weights[:768, :], mixed[...], ROWS, preferred_element_type=F32
    ).astype(BF16)


def join_kernel(keep, received, out):
    c = lax.axis_index("c")
    out[:, pl.ds(pl.multiple_of(c * 128, 128), 128)] = keep[...]
    out[:, pl.ds(pl.multiple_of((1 - c) * 128, 128), 128)] = received[...]


def shape(dims, dtype):
    return jax.ShapeDtypeStruct(dims, dtype)


def in_hbm(*values):
    return tuple(pltpu.with_memory_space_constraint(value, pltpu.HBM) for value in values)


def shards(tokens, weights, landmark_pos):
    whole = lax.all_to_all(
        jnp.broadcast_to(tokens[None], (8,) + tokens.shape), HEAD, 0, 0, tiled=True
    )
    column = lax.all_gather(weights, "z", axis=1, tiled=True).reshape(3, 16, 32, 256)
    column = call(
        stage_kernel,
        "stage",
        shape((3, 16, 32, 256), BF16),
        [VMEM],
        1 << 10,
        3 << 19,
        [pltpu.SemaphoreType.DMA((3,))],
        space=HBM,
    )(column)
    core = shift(column, "c", 1)
    column, core = in_hbm(column, core)
    landmark_pos, column = lax.optimization_barrier((landmark_pos, column))
    picked = call(
        pick_kernel,
        "pick",
        shape((8, 2048), BF16),
        [SMEM, ANY],
        1 << 20,
        1 << 19,
        [
            pltpu.VMEM((8, 8, 8, 256), BF16),
            pltpu.VMEM((8, 2048), F32),
            pltpu.SemaphoreType.DMA((8,)),
        ],
    )(landmark_pos, whole)
    picked, column, whole = lax.optimization_barrier((picked, column, whole))
    other_picked = shift(picked, "xl", 1)
    core_tokens = shift(whole, "c", 1)
    wide, packed = call(
        prepare_kernel,
        "prepare",
        (shape((2, 16, 2, 32, 256), BF16), shape((2, 3, 16, 32, 128), BF16)),
        [ANY, ANY],
        1 << 10,
        3 << 20,
        [pltpu.SemaphoreType.DMA((4,))],
    )(column, core)
    keep, give = call(
        partial_kernel,
        "partial",
        (shape((8, 128), F32), shape((8, 128), F32)),
        [VMEM, VMEM, VMEM],
        1 << 36,
        1 << 20,
    )(picked, other_picked, wide)
    packed, give = lax.optimization_barrier((packed, give))
    received = shift(give, "xl", 1)
    across = shift(packed, "xl", 1)
    spread = call(
        finish_kernel, "finish", shape((32, 8, 128), BF16), [VMEM] * 2, 1 << 34, 1 << 16
    )(keep, received)
    own_marks = lax.all_to_all(spread, CORES, 0, 0, tiled=True)
    query, keys, values, norms = call(
        project_kernel,
        "project",
        (
            shape((1536, 128), BF16),
            shape((1536, 128), BF16),
            shape((1536, 128), BF16),
            shape((1536, 1), F32),
        ),
        [VMEM, VMEM, ANY, ANY],
        2 * 1536 * 2048 * 384,
        8 << 20,
        [pltpu.VMEM((3, 16, 2, 2, 32, 128), BF16), pltpu.SemaphoreType.DMA((4,))],
    )(whole, core_tokens, packed, across)

    other_marks = shift(own_marks, "xl", 1)
    marks, chip = call(
        summary_kernel,
        "summary",
        (shape((256, 128), BF16), shape((256, 128), F32)),
        [VMEM] * 5,
        2 * 2 * 1536 * 256 * 128,
        2 << 20,
        [pltpu.VMEM((2, 256, 128), F32), pltpu.VMEM((128, 256), F32)],
        1536 * 256,
    )(own_marks, other_marks, keys, values, norms)
    chip, marks = lax.optimization_barrier((chip, marks))
    inverse = call(
        inverse_kernel,
        "inverse",
        shape((256, 256), F32),
        [VMEM],
        2 * 6 * 12 * 256**3,
        1 << 19,
        (),
        256 * 256,
    )(marks)
    pieces = lax.all_to_all(chip.reshape(32, 8, 128), CHIPS, 0, 0, tiled=True)
    spread = call(
        mixed_kernel,
        "mixed",
        shape((32, 8, 128), BF16),
        [VMEM] * 2,
        2 * 6 * 16 * 256 * 128,
        1 << 19,
    )(pieces, inverse)
    spread, marks = lax.optimization_barrier((spread, marks))
    spread = lax.all_to_all(spread, CHIPS, 0, 0, tiled=True)
    query_weights = call(
        query_weight_kernel,
        "query_weights",
        shape((1536, 256), BF16),
        [VMEM] * 2,
        2 * 1536 * 256 * 128,
        2 << 20,
        (),
        1536 * 256,
    )(query, marks)
    spread, query_weights = lax.optimization_barrier((spread, query_weights))
    mixed, give = call(
        give_kernel,
        "give",
        (shape((128, 256), BF16), shape((768, 128), BF16)),
        [VMEM] * 2,
        2 * 768 * 256 * 128,
        1 << 19,
        [pltpu.VMEM((256, 128), F32)],
    )(spread, query_weights)
    received = shift(give, "c", 1)
    keep = call(
        keep_kernel,
        "keep",
        shape((768, 128), BF16),
        [VMEM] * 2,
        2 * 768 * 256 * 128,
        1 << 19,
    )(mixed, query_weights)
    return call(
        join_kernel, "join", shape((768, 256), BF16), [VMEM] * 2, 1 << 10, 1 << 19
    )(keep, received)


def solution(mesh):
    fine = Mesh(mesh.devices.reshape(SIZES), AXES)
    return jax.shard_map(
        shards,
        mesh=fine,
        in_specs=(P(SEQ, HEAD), P(None, SEQ, HEAD), P(HEAD, None)),
        out_specs=P(SEQ, HEAD),
        check_vma=False,
    )
```

```python
import math

import jax
import jax.numpy as jnp
from jax import lax
from jax.experimental import pallas as pl
from jax.experimental.pallas import tpu as pltpu
from jax.sharding import Mesh
from jax.sharding import PartitionSpec as P

NSTEPS = 6
AXES = ("y", "xh", "z", "xl", "c")
SIZES = (4, 2, 16, 2, 2)
HEAD = ("y", "xh")
SEQ = ("z", "xl", "c")
CHIPS = ("z", "xl")
CORES = ("z", "c")

VMEM = pl.BlockSpec(memory_space=pltpu.VMEM)
SMEM = pl.BlockSpec(memory_space=pltpu.SMEM)
HBM = pl.BlockSpec(memory_space=pltpu.HBM)
ANY = pl.BlockSpec(memory_space=pl.ANY)
BF16 = jnp.bfloat16
F32 = jnp.float32
ROWS = (((1,), (1,)), ((), ()))
COLS = (((0,), (0,)), ((), ()))


def call(kernel, name, outs, ins, flops, nbytes, scratch=(), exps=0, space=VMEM):
    return pl.pallas_call(
        kernel,
        out_shape=outs,
        in_specs=ins,
        out_specs=jax.tree.map(lambda _: space, outs),
        scratch_shapes=list(scratch),
        cost_estimate=pl.CostEstimate(flops=flops, bytes_accessed=nbytes, transcendentals=exps),
        compiler_params=pltpu.CompilerParams(vmem_limit_bytes=16 << 20),
        name=name,
    )


def shift(value, axis, step):
    size = lax.axis_size(axis)
    return lax.ppermute(value, axis, [(i, (i + step) % size) for i in range(size)])


def high(left, right, dims=(((1,), (0,)), ((), ()))):
    return lax.dot_general(
        left, right, dims, precision=lax.Precision.HIGHEST, preferred_element_type=F32
    )


def side_norm(rows):
    rows32 = rows.astype(F32)
    ones = jnp.ones((8, rows.shape[1]), F32)
    return high(ones, rows32 * rows32, ROWS)[:1]


def down_norm(rows):
    rows32 = rows.astype(F32)
    return jnp.sum(rows32 * rows32, 1, keepdims=True)


def gauss(left, right, left_norm, right_norm):
    product = lax.dot_general(left, right, ROWS, preferred_element_type=F32)
    return jnp.exp((left_norm + right_norm - 2.0 * product) * (-0.5 / math.sqrt(left.shape[1])))


def run(copies):
    for copy in copies:
        copy.start()
    for copy in copies:
        copy.wait()


def stage_kernel(source, target, sems):
    run([pltpu.make_async_copy(source.at[i], target.at[i], sems.at[i]) for i in range(3)])


def pick_kernel(pos_ref, tokens, picked, groups, rows, sems):
    group = (lax.axis_index("z") * 2 + lax.axis_index("xl")) * 2 + lax.axis_index("c")
    blocks, count, width = tokens.shape
    places, copies = [], []
    for mark in range(8):
        row = pos_ref[mark // 4, group * 4 + mark % 4] - group * count
        start = pl.multiple_of((row // 8) * 8, 8)
        places.append(row - start)
        copies.append(
            pltpu.make_async_copy(
                tokens.at[:, pl.ds(start, 8), :], groups.at[mark], sems.at[mark]
            )
        )
    run(copies)
    index = lax.broadcasted_iota(jnp.int32, (8, width), 0)
    for mark, place in enumerate(places):
        for block in range(blocks):
            eight = groups[mark, block].astype(F32)
            rows[pl.ds(mark, 1), pl.ds(block * width, width)] = jnp.sum(
                jnp.where(index == place, eight, 0.0), 0, keepdims=True
            )
    picked[...] = rows[...].astype(BF16)


def prepare_kernel(column, core, w, packed, sems):
    c = lax.axis_index("c")
    cols = pl.ds(pl.multiple_of(c * 128, 128), 128)
    run(
        [
            pltpu.make_async_copy(column.at[pl.ds(0, 2)], w.at[:, :, c], sems.at[0]),
            pltpu.make_async_copy(core.at[pl.ds(0, 2)], w.at[:, :, 1 - c], sems.at[1]),
            pltpu.make_async_copy(column.at[:, :, :, cols], packed.at[c], sems.at[2]),
            pltpu.make_async_copy(core.at[:, :, :, cols], packed.at[1 - c], sems.at[3]),
        ]
    )


def partial_kernel(own, other, w, keep, give):
    xl = lax.axis_index("xl")
    rows = jnp.concatenate([own[...].astype(F32), other[...].astype(F32)], 0)
    low = lax.broadcasted_iota(jnp.int32, (16, 128), 1) < 64
    tiles = []
    for pair in range(8):
        even = rows[:, pair * 256 : pair * 256 + 128]
        odd = rows[:, pair * 256 + 128 : pair * 256 + 256]
        first = jnp.where(low, even, pltpu.roll(odd, 64, 1))
        second = jnp.where(low, pltpu.roll(even, 64, 1), odd)
        tiles.append(jnp.where(xl == 0, first, second))
    left = jnp.concatenate(tiles, 1).astype(BF16)
    results = [
        jnp.dot(left, w[kind].reshape(1024, 256), preferred_element_type=F32) for kind in range(2)
    ]
    number = lax.broadcasted_iota(jnp.int32, (16, 256), 0)
    both = jnp.where(number % 2 == 0, results[0], results[1])
    chosen = jnp.where((number[:, :128] % 8) < 4, both[:, :128], both[:, 128:])
    keep[...] = chosen[:8]
    give[...] = chosen[8:]


def finish_kernel(keep, received, spread):
    chosen = (keep[...] + received[...]).astype(BF16)
    for place in range(spread.shape[0]):
        spread[place] = chosen


def order_weights(first, packed, across, w, sems):
    xl = lax.axis_index("xl")
    copies = []
    for part in range(2):
        for source, row in ((packed, xl), (across, 1 - xl)):
            copies.append(
                pltpu.make_async_copy(
                    source.at[part, pl.ds(first, w.shape[0])],
                    w.at[:, :, row, part],
                    sems.at[len(copies)],
                )
            )
    run(copies)


def side_by_side(source, start):
    return jnp.concatenate(
        [source[block, pl.ds(start, 256), :] for block in range(source.shape[0])], 1
    )


def key_value_kernel(tokens, core_tokens, packed, across, keys, values, norms, w, sems):
    order_weights(1, packed, across, w, sems)
    blocks, rows, width = tokens.shape
    pair = jnp.concatenate([w[kind].reshape(blocks * width, 128) for kind in range(2)], 1)
    for number, source in enumerate((tokens, core_tokens)):

        @pl.loop(0, 3)
        def _(step):
            start = pl.multiple_of(step * 256, 256)
            here = pl.ds(number * rows + start, 256)
            both = jnp.dot(
                side_by_side(source, start), pair, preferred_element_type=F32
            ).astype(BF16)
            keys[here, :] = both[:, :128]
            values[here, :] = both[:, 128:]
            norms[here, :] = down_norm(both[:, :128])


def query_kernel(tokens, core_tokens, packed, across, query, w, sems):
    order_weights(0, packed, across, w, sems)
    blocks, rows, width = tokens.shape
    matrix = w[0].reshape(blocks * width, 128)
    for number, source in enumerate((tokens, core_tokens)):

        @pl.loop(0, 3)
        def _(step):
            start = pl.multiple_of(step * 256, 256)
            query[pl.ds(number * rows + start, 256), :] = jnp.dot(
                side_by_side(source, start), matrix, preferred_element_type=F32
            ).astype(BF16)


def summary_kernel(own, other, keys, values, norms, marks, pieces, flat, part):
    xl, c = lax.axis_index("xl"), lax.axis_index("c")
    flat[xl] = own[...].reshape(256, 128).astype(F32)
    flat[1 - xl] = other[...].reshape(256, 128).astype(F32)
    rows = []
    for side in range(2):
        for mark in range(4):
            first = flat[side, pl.ds(mark, 32, stride=8), :]
            second = flat[side, pl.ds(4 + mark, 32, stride=8), :]
            rows.append(jnp.where(c == 0, first, second))
    rows = jnp.concatenate(rows, 0).astype(BF16)
    marks[...] = rows
    weights = gauss(keys[...], rows, norms[...], side_norm(rows)).astype(BF16)
    part[...] = lax.dot_general(values[...], weights, COLS, preferred_element_type=F32)
    for half in range(2):
        for four in range(4):
            pieces[pl.ds(half * 4 + four, 32, stride=8), :] = part[
                pl.ds(four * 32, 32), pl.ds(half * 128, 128)
            ]


def parts(value):
    upper = value.astype(BF16)
    return upper, (value - upper.astype(F32)).astype(BF16)


def three(left, right):
    upper = jnp.dot(left[0], right[0], preferred_element_type=F32)
    cross = jnp.dot(left[0], right[1], preferred_element_type=F32)
    return upper + (cross + jnp.dot(left[1], right[0], preferred_element_type=F32))


def inverse_kernel(marks_ref, inverse_ref):
    marks = marks_ref[...]
    inner = gauss(marks, marks, down_norm(marks), side_norm(marks))
    scale_cols = jnp.max(jnp.sum(jnp.abs(inner), 0, keepdims=True), 1, keepdims=True)
    scale_rows = jnp.max(jnp.sum(jnp.abs(inner), 1, keepdims=True), 0, keepdims=True)
    iterate = inner / (scale_cols * scale_rows)
    inner = parts(inner)
    for step in range(NSTEPS):
        now = parts(iterate)
        iterate = 2.0 * iterate - three(parts(three(now, inner)), now)
    inverse_ref[...] = iterate


def mixed_kernel(pieces, inverse, spread):
    summed = jnp.sum(pieces[...], 0)
    left = high(summed, inverse[:, :128], ROWS)
    right = high(summed, inverse[:, 128:], ROWS)
    mixed = left[:4] + right[4:]
    chosen = jnp.concatenate([mixed[:, :128], mixed[:, 128:]], 0).astype(BF16)
    for place in range(spread.shape[0]):
        spread[place] = chosen


def query_weight_kernel(query, marks, weights):
    rows = marks[...]
    weights[...] = gauss(query[...], rows, down_norm(query[...]), side_norm(rows)).astype(BF16)


def give_kernel(spread, weights, mixed, give, flat):
    flat[...] = spread[...].reshape(256, 128).astype(F32)
    halves = [
        jnp.concatenate([flat[pl.ds(half * 4 + four, 32, stride=8), :] for four in range(4)], 0)
        for half in range(2)
    ]
    matrix = jnp.concatenate(halves, 1).astype(BF16)
    mixed[...] = matrix
    give[...] = lax.dot_general(
        weights[768:, :], matrix, ROWS, preferred_element_type=F32
    ).astype(BF16)


def keep_kernel(mixed, weights, keep):
    keep[...] = lax.dot_general(
        weights[:768, :], mixed[...], ROWS, preferred_element_type=F32
    ).astype(BF16)


def join_kernel(keep, received, out):
    c = lax.axis_index("c")
    out[:, pl.ds(pl.multiple_of(c * 128, 128), 128)] = keep[...]
    out[:, pl.ds(pl.multiple_of((1 - c) * 128, 128), 128)] = received[...]


def shape(dims, dtype):
    return jax.ShapeDtypeStruct(dims, dtype)


def in_hbm(*values):
    return tuple(pltpu.with_memory_space_constraint(value, pltpu.HBM) for value in values)


def shards(tokens, weights, landmark_pos):
    whole = lax.all_to_all(
        jnp.broadcast_to(tokens[None], (8,) + tokens.shape), HEAD, 0, 0, tiled=True
    )
    column = lax.all_gather(weights, "z", axis=1, tiled=True).reshape(3, 16, 32, 256)
    column = call(
        stage_kernel,
        "stage",
        shape((3, 16, 32, 256), BF16),
        [VMEM],
        1 << 10,
        3 << 19,
        [pltpu.SemaphoreType.DMA((3,))],
        space=HBM,
    )(column)
    core = shift(column, "c", 1)
    column, core = in_hbm(column, core)
    landmark_pos, column = lax.optimization_barrier((landmark_pos, column))
    picked = call(
        pick_kernel,
        "pick",
        shape((8, 2048), BF16),
        [SMEM, ANY],
        1 << 20,
        1 << 19,
        [
            pltpu.VMEM((8, 8, 8, 256), BF16),
            pltpu.VMEM((8, 2048), F32),
            pltpu.SemaphoreType.DMA((8,)),
        ],
    )(landmark_pos, whole)
    picked, column, whole = lax.optimization_barrier((picked, column, whole))
    other_picked = shift(picked, "xl", 1)
    core_tokens = shift(whole, "c", 1)
    wide, packed = call(
        prepare_kernel,
        "prepare",
        (shape((2, 16, 2, 32, 256), BF16), shape((2, 3, 16, 32, 128), BF16)),
        [ANY, ANY],
        1 << 10,
        3 << 20,
        [pltpu.SemaphoreType.DMA((4,))],
    )(column, core)
    keep, give = call(
        partial_kernel,
        "partial",
        (shape((8, 128), F32), shape((8, 128), F32)),
        [VMEM, VMEM, VMEM],
        1 << 36,
        1 << 20,
    )(picked, other_picked, wide)
    packed, give = lax.optimization_barrier((packed, give))
    received = shift(give, "xl", 1)
    across = shift(packed, "xl", 1)
    spread = call(
        finish_kernel, "finish", shape((32, 8, 128), BF16), [VMEM] * 2, 1 << 34, 1 << 16
    )(keep, received)
    own_marks = lax.all_to_all(spread, CORES, 0, 0, tiled=True)
    keys, values, norms = call(
        key_value_kernel,
        "key_values",
        (shape((1536, 128), BF16), shape((1536, 128), BF16), shape((1536, 1), F32)),
        [VMEM, VMEM, ANY, ANY],
        2 * 1536 * 2048 * 256,
        8 << 20,
        [pltpu.VMEM((2, 16, 2, 2, 32, 128), BF16), pltpu.SemaphoreType.DMA((4,))],
    )(whole, core_tokens, packed, across)
    other_marks = shift(own_marks, "xl", 1)
    marks, chip = call(
        summary_kernel,
        "summary",
        (shape((256, 128), BF16), shape((256, 128), F32)),
        [VMEM] * 5,
        2 * 2 * 1536 * 256 * 128,
        2 << 20,
        [pltpu.VMEM((2, 256, 128), F32), pltpu.VMEM((128, 256), F32)],
        1536 * 256,
    )(own_marks, other_marks, keys, values, norms)
    chip, marks = lax.optimization_barrier((chip, marks))
    inverse = call(
        inverse_kernel,
        "inverse",
        shape((256, 256), F32),
        [VMEM],
        2 * 6 * 12 * 256**3,
        1 << 19,
        (),
        256 * 256,
    )(marks)
    pieces = lax.all_to_all(chip.reshape(32, 8, 128), CHIPS, 0, 0, tiled=True)
    spread = call(
        mixed_kernel,
        "mixed",
        shape((32, 8, 128), BF16),
        [VMEM] * 2,
        2 * 6 * 16 * 256 * 128,
        1 << 19,
    )(pieces, inverse)
    spread, marks, packed = lax.optimization_barrier((spread, marks, packed))
    spread = lax.all_to_all(spread, CHIPS, 0, 0, tiled=True)
    query = call(
        query_kernel,
        "queries",
        shape((1536, 128), BF16),
        [VMEM, VMEM, ANY, ANY],
        2 * 1536 * 2048 * 128,
        7 << 20,
        [pltpu.VMEM((1, 16, 2, 2, 32, 128), BF16), pltpu.SemaphoreType.DMA((4,))],
    )(whole, core_tokens, packed, across)
    query_weights = call(
        query_weight_kernel,
        "query_weights",
        shape((1536, 256), BF16),
        [VMEM] * 2,
        2 * 1536 * 256 * 128,
        2 << 20,
        (),
        1536 * 256,
    )(query, marks)
    spread, query_weights = lax.optimization_barrier((spread, query_weights))
    mixed, give = call(
        give_kernel,
        "give",
        (shape((128, 256), BF16), shape((768, 128), BF16)),
        [VMEM] * 2,
        2 * 768 * 256 * 128,
        1 << 19,
        [pltpu.VMEM((256, 128), F32)],
    )(spread, query_weights)
    received = shift(give, "c", 1)
    keep = call(
        keep_kernel,
        "keep",
        shape((768, 128), BF16),
        [VMEM] * 2,
        2 * 768 * 256 * 128,
        1 << 19,
    )(mixed, query_weights)
    return call(
        join_kernel, "join", shape((768, 256), BF16), [VMEM] * 2, 1 << 10, 1 << 19
    )(keep, received)


def solution(mesh):
    fine = Mesh(mesh.devices.reshape(SIZES), AXES)
    return jax.shard_map(
        shards,
        mesh=fine,
        in_specs=(P(SEQ, HEAD), P(None, SEQ, HEAD), P(HEAD, None)),
        out_specs=P(SEQ, HEAD),
        check_vma=False,
    )
```

```python
import math

import jax
import jax.numpy as jnp
from jax import lax
from jax.experimental import pallas as pl
from jax.experimental.pallas import tpu as pltpu
from jax.sharding import Mesh
from jax.sharding import PartitionSpec as P

NSTEPS = 6
AXES = ("y", "xh", "z", "xl", "c")
SIZES = (4, 2, 16, 2, 2)
HEAD = ("y", "xh")
SEQ = ("z", "xl", "c")
CHIPS = ("z", "xl")
CORES = ("z", "c")

VMEM = pl.BlockSpec(memory_space=pltpu.VMEM)
SMEM = pl.BlockSpec(memory_space=pltpu.SMEM)
HBM = pl.BlockSpec(memory_space=pltpu.HBM)
ANY = pl.BlockSpec(memory_space=pl.ANY)
BF16 = jnp.bfloat16
F32 = jnp.float32
ROWS = (((1,), (1,)), ((), ()))
COLS = (((0,), (0,)), ((), ()))


def call(kernel, name, outs, ins, flops, nbytes, scratch=(), exps=0, space=VMEM):
    return pl.pallas_call(
        kernel,
        out_shape=outs,
        in_specs=ins,
        out_specs=jax.tree.map(lambda _: space, outs),
        scratch_shapes=list(scratch),
        cost_estimate=pl.CostEstimate(flops=flops, bytes_accessed=nbytes, transcendentals=exps),
        compiler_params=pltpu.CompilerParams(vmem_limit_bytes=16 << 20),
        name=name,
    )


def shift(value, axis, step):
    size = lax.axis_size(axis)
    return lax.ppermute(value, axis, [(i, (i + step) % size) for i in range(size)])


def high(left, right, dims=(((1,), (0,)), ((), ()))):
    return lax.dot_general(
        left, right, dims, precision=lax.Precision.HIGHEST, preferred_element_type=F32
    )


def side_norm(rows):
    rows32 = rows.astype(F32)
    ones = jnp.ones((8, rows.shape[1]), F32)
    return high(ones, rows32 * rows32, ROWS)[:1]


def down_norm(rows):
    rows32 = rows.astype(F32)
    return jnp.sum(rows32 * rows32, 1, keepdims=True)


def gauss(left, right, left_norm, right_norm):
    product = lax.dot_general(left, right, ROWS, preferred_element_type=F32)
    return jnp.exp((left_norm + right_norm - 2.0 * product) * (-0.5 / math.sqrt(left.shape[1])))


def run(copies):
    for copy in copies:
        copy.start()
    for copy in copies:
        copy.wait()


def stage_kernel(source, target, sems):
    run([pltpu.make_async_copy(source.at[i], target.at[i], sems.at[i]) for i in range(3)])


def pick_kernel(pos_ref, tokens, picked, groups, rows, sems):
    group = (lax.axis_index("z") * 2 + lax.axis_index("xl")) * 2 + lax.axis_index("c")
    blocks, count, width = tokens.shape
    places, copies = [], []
    for mark in range(8):
        row = pos_ref[mark // 4, group * 4 + mark % 4] - group * count
        start = pl.multiple_of((row // 8) * 8, 8)
        places.append(row - start)
        copies.append(
            pltpu.make_async_copy(
                tokens.at[:, pl.ds(start, 8), :], groups.at[mark], sems.at[mark]
            )
        )
    run(copies)
    index = lax.broadcasted_iota(jnp.int32, (8, width), 0)
    for mark, place in enumerate(places):
        for block in range(blocks):
            eight = groups[mark, block].astype(F32)
            rows[pl.ds(mark, 1), pl.ds(block * width, width)] = jnp.sum(
                jnp.where(index == place, eight, 0.0), 0, keepdims=True
            )
    picked[...] = rows[...].astype(BF16)


def prepare_kernel(column, core, w, packed, sems):
    c = lax.axis_index("c")
    cols = pl.ds(pl.multiple_of(c * 128, 128), 128)
    run(
        [
            pltpu.make_async_copy(column.at[pl.ds(0, 2)], w.at[:, :, c], sems.at[0]),
            pltpu.make_async_copy(core.at[pl.ds(0, 2)], w.at[:, :, 1 - c], sems.at[1]),
            pltpu.make_async_copy(column.at[:, :, :, cols], packed.at[c], sems.at[2]),
            pltpu.make_async_copy(core.at[:, :, :, cols], packed.at[1 - c], sems.at[3]),
        ]
    )


def partial_kernel(own, other, w, keep, give):
    xl = lax.axis_index("xl")
    rows = jnp.concatenate([own[...].astype(F32), other[...].astype(F32)], 0)
    low = lax.broadcasted_iota(jnp.int32, (16, 128), 1) < 64
    tiles = []
    for pair in range(8):
        even = rows[:, pair * 256 : pair * 256 + 128]
        odd = rows[:, pair * 256 + 128 : pair * 256 + 256]
        first = jnp.where(low, even, pltpu.roll(odd, 64, 1))
        second = jnp.where(low, pltpu.roll(even, 64, 1), odd)
        tiles.append(jnp.where(xl == 0, first, second))
    left = jnp.concatenate(tiles, 1).astype(BF16)
    results = [
        jnp.dot(left, w[kind].reshape(1024, 256), preferred_element_type=F32) for kind in range(2)
    ]
    number = lax.broadcasted_iota(jnp.int32, (16, 256), 0)
    both = jnp.where(number % 2 == 0, results[0], results[1])
    chosen = jnp.where((number[:, :128] % 8) < 4, both[:, :128], both[:, 128:])
    keep[...] = chosen[:8]
    give[...] = chosen[8:]


def finish_kernel(keep, received, spread):
    chosen = (keep[...] + received[...]).astype(BF16)
    for place in range(spread.shape[0]):
        spread[place] = chosen


def order_weights(first, packed, across, w, sems):
    xl = lax.axis_index("xl")
    copies = []
    for part in range(2):
        for source, row in ((packed, xl), (across, 1 - xl)):
            copies.append(
                pltpu.make_async_copy(
                    source.at[part, pl.ds(first, w.shape[0])],
                    w.at[:, :, row, part],
                    sems.at[len(copies)],
                )
            )
    run(copies)


def side_by_side(source, start):
    return jnp.concatenate(
        [source[block, pl.ds(start, 256), :] for block in range(source.shape[0])], 1
    )


def key_value_kernel(tokens, core_tokens, packed, across, keys, values, norms, w, sems):
    order_weights(1, packed, across, w, sems)
    blocks, rows, width = tokens.shape
    pair = jnp.concatenate([w[kind].reshape(blocks * width, 128) for kind in range(2)], 1)
    for number, source in enumerate((tokens, core_tokens)):

        @pl.loop(0, 3)
        def _(step):
            start = pl.multiple_of(step * 256, 256)
            here = pl.ds(number * rows + start, 256)
            both = jnp.dot(
                side_by_side(source, start), pair, preferred_element_type=F32
            ).astype(BF16)
            keys[here, :] = both[:, :128]
            values[here, :] = both[:, 128:]
            norms[here, :] = down_norm(both[:, :128])


def query_kernel(tokens, core_tokens, packed, across, query, w, sems):
    order_weights(0, packed, across, w, sems)
    blocks, rows, width = tokens.shape
    matrix = w[0].reshape(blocks * width, 128)
    for number, source in enumerate((tokens, core_tokens)):

        @pl.loop(0, 3)
        def _(step):
            start = pl.multiple_of(step * 256, 256)
            query[pl.ds(number * rows + start, 256), :] = jnp.dot(
                side_by_side(source, start), matrix, preferred_element_type=F32
            ).astype(BF16)


def summary_kernel(own, other, keys, values, norms, marks, pieces, flat, part):
    xl, c = lax.axis_index("xl"), lax.axis_index("c")
    flat[xl] = own[...].reshape(256, 128).astype(F32)
    flat[1 - xl] = other[...].reshape(256, 128).astype(F32)
    rows = []
    for side in range(2):
        for mark in range(4):
            first = flat[side, pl.ds(mark, 32, stride=8), :]
            second = flat[side, pl.ds(4 + mark, 32, stride=8), :]
            rows.append(jnp.where(c == 0, first, second))
    rows = jnp.concatenate(rows, 0).astype(BF16)
    marks[...] = rows
    weights = gauss(keys[...], rows, norms[...], side_norm(rows)).astype(BF16)
    part[...] = lax.dot_general(values[...], weights, COLS, preferred_element_type=F32)
    for half in range(2):
        for four in range(4):
            pieces[pl.ds(half * 4 + four, 32, stride=8), :] = part[
                pl.ds(four * 32, 32), pl.ds(half * 128, 128)
            ]


def parts(value):
    upper = value.astype(BF16)
    return upper, (value - upper.astype(F32)).astype(BF16)


def three(left, right):
    upper = jnp.dot(left[0], right[0], preferred_element_type=F32)
    cross = jnp.dot(left[0], right[1], preferred_element_type=F32)
    return upper + (cross + jnp.dot(left[1], right[0], preferred_element_type=F32))


def inverse_kernel(marks_ref, inverse_ref):
    marks = marks_ref[...]
    inner = gauss(marks, marks, down_norm(marks), side_norm(marks))
    scale_cols = jnp.max(jnp.sum(jnp.abs(inner), 0, keepdims=True), 1, keepdims=True)
    scale_rows = jnp.max(jnp.sum(jnp.abs(inner), 1, keepdims=True), 0, keepdims=True)
    iterate = inner / (scale_cols * scale_rows)
    inner = parts(inner)
    for step in range(NSTEPS):
        now = parts(iterate)
        iterate = 2.0 * iterate - three(parts(three(now, inner)), now)
    inverse_ref[...] = iterate


def mixed_kernel(pieces, inverse, spread):
    summed = jnp.sum(pieces[...], 0)
    left = high(summed, inverse[:, :128], ROWS)
    right = high(summed, inverse[:, 128:], ROWS)
    mixed = left[:4] + right[4:]
    chosen = jnp.concatenate([mixed[:, :128], mixed[:, 128:]], 0).astype(BF16)
    for place in range(spread.shape[0]):
        spread[place] = chosen


def query_weight_kernel(query, marks, weights):
    rows = marks[...]
    weights[...] = gauss(query[...], rows, down_norm(query[...]), side_norm(rows)).astype(BF16)


def give_kernel(spread, weights, mixed, give, flat):
    flat[...] = spread[...].reshape(256, 128).astype(F32)
    halves = [
        jnp.concatenate([flat[pl.ds(half * 4 + four, 32, stride=8), :] for four in range(4)], 0)
        for half in range(2)
    ]
    matrix = jnp.concatenate(halves, 1).astype(BF16)
    mixed[...] = matrix
    give[...] = lax.dot_general(
        weights[768:, :], matrix, ROWS, preferred_element_type=F32
    ).astype(BF16)


def keep_kernel(mixed, weights, out):
    c = lax.axis_index("c")
    out[:, pl.ds(pl.multiple_of(c * 128, 128), 128)] = lax.dot_general(
        weights[:768, :], mixed[...], ROWS, preferred_element_type=F32
    ).astype(BF16)


def join_kernel(begun, received, out, sems):
    c = lax.axis_index("c")
    cols = pl.ds(pl.multiple_of((1 - c) * 128, 128), 128)
    run(
        [
            pltpu.make_async_copy(
                received.at[pl.ds(i * 192, 192)], out.at[pl.ds(i * 192, 192), cols], sems.at[i]
            )
            for i in range(4)
        ]
    )


def shape(dims, dtype):
    return jax.ShapeDtypeStruct(dims, dtype)


def in_hbm(*values):
    return tuple(pltpu.with_memory_space_constraint(value, pltpu.HBM) for value in values)


def shards(tokens, weights, landmark_pos):
    whole = lax.all_to_all(
        jnp.broadcast_to(tokens[None], (8,) + tokens.shape), HEAD, 0, 0, tiled=True
    )
    column = lax.all_gather(weights, "z", axis=1, tiled=True).reshape(3, 16, 32, 256)
    column = call(
        stage_kernel,
        "stage",
        shape((3, 16, 32, 256), BF16),
        [VMEM],
        1 << 10,
        3 << 19,
        [pltpu.SemaphoreType.DMA((3,))],
        space=HBM,
    )(column)
    core = shift(column, "c", 1)
    column, core = in_hbm(column, core)
    landmark_pos, column = lax.optimization_barrier((landmark_pos, column))
    picked = call(
        pick_kernel,
        "pick",
        shape((8, 2048), BF16),
        [SMEM, ANY],
        1 << 20,
        1 << 19,
        [
            pltpu.VMEM((8, 8, 8, 256), BF16),
            pltpu.VMEM((8, 2048), F32),
            pltpu.SemaphoreType.DMA((8,)),
        ],
    )(landmark_pos, whole)
    picked, column, whole = lax.optimization_barrier((picked, column, whole))
    other_picked = shift(picked, "xl", 1)
    core_tokens = shift(whole, "c", 1)
    wide, packed = call(
        prepare_kernel,
        "prepare",
        (shape((2, 16, 2, 32, 256), BF16), shape((2, 3, 16, 32, 128), BF16)),
        [ANY, ANY],
        1 << 10,
        3 << 20,
        [pltpu.SemaphoreType.DMA((4,))],
    )(column, core)
    keep, give = call(
        partial_kernel,
        "partial",
        (shape((8, 128), F32), shape((8, 128), F32)),
        [VMEM, VMEM, VMEM],
        1 << 36,
        1 << 20,
    )(picked, other_picked, wide)
    packed, give = lax.optimization_barrier((packed, give))
    received = shift(give, "xl", 1)
    across = shift(packed, "xl", 1)
    spread = call(
        finish_kernel, "finish", shape((32, 8, 128), BF16), [VMEM] * 2, 1 << 34, 1 << 16
    )(keep, received)
    own_marks = lax.all_to_all(spread, CORES, 0, 0, tiled=True)
    keys, values, norms = call(
        key_value_kernel,
        "key_values",
        (shape((1536, 128), BF16), shape((1536, 128), BF16), shape((1536, 1), F32)),
        [VMEM, VMEM, ANY, ANY],
        2 * 1536 * 2048 * 256,
        8 << 20,
        [pltpu.VMEM((2, 16, 2, 2, 32, 128), BF16), pltpu.SemaphoreType.DMA((4,))],
    )(whole, core_tokens, packed, across)
    other_marks = shift(own_marks, "xl", 1)
    marks, chip = call(
        summary_kernel,
        "summary",
        (shape((256, 128), BF16), shape((256, 128), F32)),
        [VMEM] * 5,
        2 * 2 * 1536 * 256 * 128,
        2 << 20,
        [pltpu.VMEM((2, 256, 128), F32), pltpu.VMEM((128, 256), F32)],
        1536 * 256,
    )(own_marks, other_marks, keys, values, norms)
    chip, marks = lax.optimization_barrier((chip, marks))
    inverse = call(
        inverse_kernel,
        "inverse",
        shape((256, 256), F32),
        [VMEM],
        2 * 6 * 12 * 256**3,
        1 << 19,
        (),
        256 * 256,
    )(marks)
    pieces = lax.all_to_all(chip.reshape(32, 8, 128), CHIPS, 0, 0, tiled=True)
    spread = call(
        mixed_kernel,
        "mixed",
        shape((32, 8, 128), BF16),
        [VMEM] * 2,
        2 * 6 * 16 * 256 * 128,
        1 << 19,
    )(pieces, inverse)
    spread, marks, packed = lax.optimization_barrier((spread, marks, packed))
    spread = lax.all_to_all(spread, CHIPS, 0, 0, tiled=True)
    query = call(
        query_kernel,
        "queries",
        shape((1536, 128), BF16),
        [VMEM, VMEM, ANY, ANY],
        2 * 1536 * 2048 * 128,
        7 << 20,
        [pltpu.VMEM((1, 16, 2, 2, 32, 128), BF16), pltpu.SemaphoreType.DMA((4,))],
    )(whole, core_tokens, packed, across)
    query_weights = call(
        query_weight_kernel,
        "query_weights",
        shape((1536, 256), BF16),
        [VMEM] * 2,
        2 * 1536 * 256 * 128,
        2 << 20,
        (),
        1536 * 256,
    )(query, marks)
    spread, query_weights = lax.optimization_barrier((spread, query_weights))
    mixed, give = call(
        give_kernel,
        "give",
        (shape((128, 256), BF16), shape((768, 128), BF16)),
        [VMEM] * 2,
        2 * 768 * 256 * 128,
        1 << 19,
        [pltpu.VMEM((256, 128), F32)],
    )(spread, query_weights)
    received = shift(give, "c", 1)
    keep = call(
        keep_kernel,
        "keep",
        shape((768, 256), BF16),
        [VMEM] * 2,
        2 * 768 * 256 * 128,
        1 << 19,
    )(mixed, query_weights)
    return pl.pallas_call(
        join_kernel,
        out_shape=shape((768, 256), BF16),
        in_specs=[ANY, VMEM],
        out_specs=ANY,
        scratch_shapes=[pltpu.SemaphoreType.DMA((4,))],
        input_output_aliases={0: 0},
        cost_estimate=pl.CostEstimate(flops=1 << 10, bytes_accessed=1 << 19, transcendentals=0),
        name="join",
    )(keep, received)


def solution(mesh):
    fine = Mesh(mesh.devices.reshape(SIZES), AXES)
    return jax.shard_map(
        shards,
        mesh=fine,
        in_specs=(P(SEQ, HEAD), P(None, SEQ, HEAD), P(HEAD, None)),
        out_specs=P(SEQ, HEAD),
        check_vma=False,
    )
```
